256 devices in a mesh: ma: 32 (over z, x_lo, core), bl: 8 (over y, x_hi).
Axes of the slice: x: 4 (x_hi: 2, x_lo: 2; x = x_hi * 2 + x_lo), y: 4, z: 8, core: 2. Of those that a mesh axis runs over, the one named last changes fastest.
Arguments:
- visibilities: bfloat16 [2, 16640, 8192], P(None, 'bl', 'ma'), may hold values from -6 to 6
- beam_blocks: bfloat16 [32, 2, 16640, 1000], P('ma', None, 'bl'), may hold values from -0.0625 to 0.0625
- feed_pairs: int32 [16640, 2], P('bl'), may hold values from 0 to 1023
- feed_gains: float32 [2, 1024], replicated, may hold values from -1.5 to 1.5
- m_order: int32 [32], replicated, may hold values from 0 to 31, each once
Outputs:
- sky_modes: float32 [2, 32, 1000], P(None, 'ma', 'bl')
The draws below stay inside these ranges and needn't reach their ends.
All inputs are finite; a program needn't handle non-finite values.
Results may differ from the reference program's by a relative error of at most 0.0049.
Values may be sent and summed in bfloat16 or wider, within the bound.
No kernel may reach another device: no remote copies, remote signals or barrier semaphores. Data moves between devices by JAX's collectives and lax.ppermute only.
A program may use at most 64 MiB of HBM per device.

```python
import jax
import jax.numpy as jnp
from jax import lax

NT = 8192
L = 1000
NFEED = 1024
NB = 16640
M = 32


def with_ends(values, key, low, top_value):
    place = [jax.random.randint(jax.random.fold_in(key, axis), (), 0, length) for axis, length in enumerate(values.shape)]
    main_axis = values.shape.index(max(values.shape))
    neighbour = place[:main_axis] + [(place[main_axis] + 1) % values.shape[main_axis]] + place[main_axis + 1:]
    return values.at[tuple(place)].set(low).at[tuple(neighbour)].set(top_value)


def with_spikes(drawn, rng, source, target, shards_of, factor):
    def block_of(position):
        return (jnp.arange(drawn.shape[position]) // (drawn.shape[position] // shards_of)).reshape((-1,) + (1,) * (drawn.ndim - 1 - position))

    near = jax.random.permutation(rng, shards_of)[block_of(target)]
    other_side = (block_of(target) + shards_of // 2) % shards_of
    return jnp.where((block_of(source) == near) | (block_of(source) == other_side), factor * drawn, drawn)


def block_levels(own_key, extent, cuts, smallest, high):
    loudness = 1.0
    for position, shards_of in cuts:
        draws = jax.random.uniform(jax.random.fold_in(jax.random.fold_in(own_key, 6), position), (shards_of,), jnp.float32, smallest / len(cuts), high / len(cuts))
        loudness = loudness * jnp.repeat(jnp.exp(draws), extent[position] // shards_of).reshape((-1,) + (1,) * (len(extent) - 1 - position))
    return loudness


def centred(own_key, shape, spread, reach, split=(), kind=jnp.bfloat16):
    array = jax.random.normal(own_key, shape, jnp.float32) * spread
    if len(split) > 0:
        array = block_levels(own_key, shape, split, -0.22, 0.18) * array
    return jnp.clip(array, min=-reach, max=reach).astype(kind)


def noise_with(key, dims, scale, most, pieces, heavy, kind=jnp.bfloat16):
    values = scale * jax.random.normal(key, dims, jnp.float32)
    if pieces:
        values = values * block_levels(key, dims, pieces, -0.22, 0.18)
    return jnp.clip(with_spikes(values, jax.random.fold_in(key, 3), *heavy), -most, most).astype(kind)


def setup_inputs(seed: int = 0) -> dict:
    keys = jax.random.split(jax.random.key(seed), 6)
    visibilities = centred(keys[0], (2, NB, NT), 1.0, 6.0, ((1, 8), (2, 32)))
    beam_blocks = noise_with(keys[1], (M, 2, NB, L), NB ** -0.5, 0.0625, ((0, 32), (2, 8)), (2, 3, 8, 2.0))
    feed_pairs = with_ends(jax.random.randint(keys[2], (NB, 2), 0, NFEED), jax.random.fold_in(keys[2], 1), 0, NFEED - 1).astype(jnp.int32)
    feed_gains = jnp.clip(jax.random.uniform(keys[3], (2, NFEED), jnp.float32, -1.5, 1.5), -1.5, 1.5)
    m_order = jax.random.permutation(keys[4], M).astype(jnp.int32)
    return dict(visibilities=visibilities, beam_blocks=beam_blocks, feed_pairs=feed_pairs, feed_gains=feed_gains, m_order=m_order)


def dft_weights(time_index, m_values):
    wrapped = jnp.mod(time_index[:, None] * m_values[None, :], NT).astype(jnp.float32)
    phases = wrapped * (2.0 * jnp.pi / NT)
    scale = 1.0 / jnp.sqrt(jnp.float32(NT))
    cos_part = (jnp.cos(phases) * scale).astype(jnp.bfloat16)
    sin_part = (jnp.sin(phases) * scale).astype(jnp.bfloat16)
    upper = jnp.concatenate([cos_part, -sin_part], axis=1)
    lower = jnp.concatenate([sin_part, cos_part], axis=1)
    return jnp.concatenate([upper, lower], axis=0)

def reference(visibilities, beam_blocks, feed_pairs, feed_gains, m_order):
    count = m_order.shape[0]
    m_values = (m_order - count // 2).astype(jnp.int32)
    time_index = jnp.arange(NT, dtype=jnp.int32)
    weights = dft_weights(time_index, m_values)
    stacked_in = jnp.concatenate([visibilities[0], visibilities[1]], axis=1)
    spectra_flat = jnp.dot(stacked_in, weights, preferred_element_type=jnp.float32)
    spectra = jnp.stack([spectra_flat[:, :count], spectra_flat[:, count:]]).astype(jnp.bfloat16)
    first_feed = feed_pairs[:, 0]
    second_feed = feed_pairs[:, 1]
    gain_re = feed_gains[0]
    gain_im = feed_gains[1]
    a_re = gain_re[first_feed]
    a_im = gain_im[first_feed]
    b_re = gain_re[second_feed]
    b_im = gain_im[second_feed]
    factor_re = (a_re * b_re + a_im * b_im)[:, None]
    factor_im = (a_im * b_re - a_re * b_im)[:, None]
    spec_re = spectra[0].astype(jnp.float32)
    spec_im = spectra[1].astype(jnp.float32)
    weighted_re = (spec_re * factor_re - spec_im * factor_im).astype(jnp.bfloat16)
    weighted_im = (spec_re * factor_im + spec_im * factor_re).astype(jnp.bfloat16)
    row_real = jnp.concatenate([weighted_re, weighted_im], axis=0)
    row_imag = jnp.concatenate([weighted_im, -weighted_re], axis=0)
    vectors = jnp.stack([row_real, row_imag])
    vectors = jnp.transpose(vectors, (2, 0, 1))
    total_rows = beam_blocks.shape[2]
    width = beam_blocks.shape[3]

    def project(pair):
        vector, block = pair
        flat_block = block.reshape(2 * total_rows, width)
        return jnp.dot(vector, flat_block, preferred_element_type=jnp.float32)
    result = lax.map(project, (vectors, beam_blocks))
    return jnp.transpose(result, (1, 0, 2))
```

```python
import jax
import jax.numpy as jnp
from jax import lax
from jax.experimental import pallas as pl
from jax.experimental.pallas import tpu as pltpu
from jax.sharding import PartitionSpec as P

NT = 8192
GROUPS = 4
LANES = 128


def group_spans(rows):
    step = rows // GROUPS // LANES * LANES
    starts = [group * step for group in range(GROUPS)]
    return [(start, (starts[i + 1] if i + 1 < GROUPS else rows) - start) for i, start in enumerate(starts)]


def lane_pieces(size):
    return [(at, min(LANES, size - at)) for at in range(0, size, LANES)]


def padded(size):
    return -(-size // LANES) * LANES


def transform_kernel(spans, first_time, m_ref, vis_ref, out_ref, held, lines, sems):
    copies = []
    for group, (start, size) in enumerate(spans):
        rows = pl.ds(start, size)
        copy = pltpu.make_async_copy(vis_ref.at[:, rows, :], held.at[:, rows, :], sems.at[group])
        copy.start()
        copies.append(copy)
    count = m_ref.shape[0]
    times = vis_ref.shape[2]
    slot = lax.broadcasted_iota(jnp.int32, (count, LANES), 0)
    m_values = jnp.zeros((count, LANES), jnp.int32)
    for j in range(count):
        m_values = jnp.where(slot == j, m_ref[j] - count // 2, m_values)
    begin = first_time() * times
    scale = 1.0 / jnp.sqrt(jnp.float32(NT))
    cos_parts, sin_parts = [], []
    for at in range(0, times, LANES):
        t = begin + at + lax.broadcasted_iota(jnp.int32, (count, LANES), 1)
        wrapped = jnp.bitwise_and(t * m_values, NT - 1).astype(jnp.float32)
        phases = wrapped * (2.0 * jnp.pi / NT)
        cos_parts.append(jnp.cos(phases) * scale)
        sin_parts.append(jnp.sin(phases) * scale)
    cos_part = jnp.concatenate(cos_parts, axis=1)
    sin_part = jnp.concatenate(sin_parts, axis=1)
    for_real = jnp.concatenate([cos_part, -sin_part], axis=0).astype(jnp.bfloat16)
    for_imag = jnp.concatenate([sin_part, cos_part], axis=0).astype(jnp.bfloat16)
    lines[...] = jnp.zeros_like(lines)
    contract = (((1,), (1,)), ((), ()))
    for group, (start, size) in enumerate(spans):
        copies[group].wait()
        rows = pl.ds(start, size)
        found = lax.dot_general(for_real, held[0, rows, :], contract, preferred_element_type=jnp.float32)
        found += lax.dot_general(for_imag, held[1, rows, :], contract, preferred_element_type=jnp.float32)
        for piece, (at, width) in enumerate(lane_pieces(size)):
            for part in range(2):
                lines[piece, pl.ds(part * GROUPS + group, count, stride=2 * GROUPS), :width] = found[
                    part * count:(part + 1) * count, at:at + width
                ]
    for piece in range(lines.shape[0]):
        block = lines[piece].reshape(count, 2 * GROUPS, LANES)
        out_ref[:, :, piece * LANES:(piece + 1) * LANES] = block.astype(jnp.bfloat16)


def transform(visibilities, m_order, axis):
    rows, times = visibilities.shape[1:]
    count = m_order.shape[0]
    spans = group_spans(rows)
    width = padded(max(size for _, size in spans))

    def body(begin_ref, *refs):
        transform_kernel(spans, lambda: begin_ref[0], *refs)

    return pl.pallas_call(
        body,
        out_shape=jax.ShapeDtypeStruct((count, 2 * GROUPS, width), jnp.bfloat16),
        in_specs=[
            pl.BlockSpec(memory_space=pltpu.SMEM),
            pl.BlockSpec(memory_space=pltpu.SMEM),
            pl.BlockSpec(memory_space=pl.ANY),
        ],
        out_specs=pl.BlockSpec(memory_space=pltpu.VMEM),
        scratch_shapes=[
            pltpu.VMEM((2, rows, times), jnp.bfloat16),
            pltpu.VMEM((width // LANES, count * 2 * GROUPS, LANES), jnp.float32),
            pltpu.SemaphoreType.DMA((GROUPS,)),
        ],
        name="transform",
    )(lax.axis_index(axis).reshape(1), m_order, visibilities)


def three_pieces(value):
    first = value.astype(jnp.bfloat16)
    rest = value - first.astype(jnp.float32)
    second = rest.astype(jnp.bfloat16)
    third = (rest - second.astype(jnp.float32)).astype(jnp.bfloat16)
    return [first, second, third]


def factor_kernel(spans, pairs_ref, gains_ref, out_ref):
    feeds = gains_ref.shape[1]
    tiles = feeds // LANES
    table = jnp.concatenate(
        [gains_ref[part:part + 1, tile * LANES:(tile + 1) * LANES] for part in range(2) for tile in range(tiles)], axis=0
    )
    pieces = jnp.concatenate(three_pieces(table), axis=0)
    tall = 2 * tiles
    out_ref[...] = jnp.zeros_like(out_ref)
    for group, (start, size) in enumerate(spans):
        picked = []
        for side in range(2):
            feed = pairs_ref[side:side + 1, pl.ds(start, size)]
            lane = jnp.bitwise_and(feed, LANES - 1)
            tile = lax.shift_right_logical(feed, LANES.bit_length() - 1)
            lane_iota = lax.broadcasted_iota(jnp.int32, (LANES, size), 0)
            one_hot = jnp.where(lane_iota == lane, 1.0, 0.0).astype(jnp.bfloat16)
            rows = jnp.dot(pieces, one_hot, preferred_element_type=jnp.float32)
            whole = (rows[:tall] + rows[tall:2 * tall]) + rows[2 * tall:]
            chosen = lax.broadcasted_iota(jnp.int32, (tiles, size), 0) == tile
            for part in range(2):
                picked.append(jnp.sum(jnp.where(chosen, whole[part * tiles:(part + 1) * tiles], 0.0), axis=0, keepdims=True))
        a_re, a_im, b_re, b_im = picked
        factor_re = a_re * b_re + a_im * b_im
        factor_im = a_im * b_re - a_re * b_im
        out_ref[0, group:group + 1, :size] = factor_re
        out_ref[0, GROUPS + group:GROUPS + group + 1, :size] = factor_re
        out_ref[1, group:group + 1, :size] = -factor_im
        out_ref[1, GROUPS + group:GROUPS + group + 1, :size] = factor_im


def factors(feed_pairs, feed_gains):
    rows = feed_pairs.shape[0]
    spans = group_spans(rows)
    width = padded(max(size for _, size in spans))

    def body(*refs):
        factor_kernel(spans, *refs)

    return pl.pallas_call(
        body,
        out_shape=jax.ShapeDtypeStruct((2, 2 * GROUPS, width), jnp.float32),
        in_specs=[pl.BlockSpec(memory_space=pltpu.VMEM)] * 2,
        out_specs=pl.BlockSpec(memory_space=pltpu.VMEM),
        cost_estimate=pl.CostEstimate(flops=2 * 2 * rows * 48 * 128, bytes_accessed=rows * 8 + 8192 + 40960, transcendentals=0),
        name="factors",
    )(jnp.transpose(feed_pairs), feed_gains)


def project_kernel(spans, shares, got_ref, factor_ref, beam_ref, out_ref, held, sems):
    copies = []
    for part in range(2):
        for group, (start, size) in enumerate(spans):
            rows = pl.ds(start, size)
            copy = pltpu.make_async_copy(
                beam_ref.at[0, part, rows, :], held.at[part, rows, :], sems.at[part * GROUPS + group]
            )
            copy.start()
            copies.append(copy)
    total = got_ref[0].astype(jnp.float32)
    for source in range(1, got_ref.shape[0]):
        total += got_ref[source].astype(jnp.float32)
    swapped = jnp.concatenate([total[GROUPS:], total[:GROUPS]], axis=0)
    weighted = total * factor_ref[0] + swapped * factor_ref[1]
    high = weighted.astype(jnp.bfloat16)
    low = (weighted - high.astype(jnp.float32)).astype(jnp.bfloat16)
    rows16 = jnp.concatenate([high.astype(jnp.float32), low.astype(jnp.float32)], axis=0)
    row_group = jnp.bitwise_and(lax.broadcasted_iota(jnp.int32, rows16.shape, 0), GROUPS - 1)
    lefts = [jnp.where(row_group == group, rows16, 0.0).astype(jnp.bfloat16) for group in range(GROUPS)]
    sums = []
    for part in range(2):
        value = None
        for group, (start, size) in enumerate(spans):
            copies[part * GROUPS + group].wait()
            term = jnp.dot(lefts[group][:, :size], held[part, pl.ds(start, size), :], preferred_element_type=jnp.float32)
            value = term if value is None else value + term
        value = value[:2 * GROUPS] + value[2 * GROUPS:]
        sums.append(
            [jnp.sum(value[piece * GROUPS:(piece + 1) * GROUPS], axis=0, keepdims=True) for piece in range(2)]
        )
    answer = jnp.concatenate([sums[0][0] + sums[1][1], sums[0][1] - sums[1][0]], axis=0)
    width = answer.shape[1]
    share = width // shares
    for k in range(shares):
        out_ref[k, :, :share] = answer[:, k * share:(k + 1) * share]


def project(got, factor, beam_blocks, shares):
    rows, width = beam_blocks.shape[2:]
    spans = group_spans(rows)

    def body(*refs):
        project_kernel(spans, shares, *refs)

    return pl.pallas_call(
        body,
        out_shape=jax.ShapeDtypeStruct((shares, 2, padded(width // shares)), jnp.float32),
        in_specs=[
            pl.BlockSpec(memory_space=pltpu.VMEM),
            pl.BlockSpec(memory_space=pltpu.VMEM),
            pl.BlockSpec(memory_space=pl.ANY),
        ],
        out_specs=pl.BlockSpec(memory_space=pltpu.VMEM),
        scratch_shapes=[
            pltpu.VMEM((2, rows, width), jnp.bfloat16),
            pltpu.SemaphoreType.DMA((2 * GROUPS,)),
        ],
        compiler_params=pltpu.CompilerParams(vmem_limit_bytes=32 * 1024 * 1024),
        name="project",
    )(got, factor, beam_blocks)


def per_device(visibilities, beam_blocks, feed_pairs, feed_gains, m_order):
    shares = lax.axis_size("bl")
    share_width = beam_blocks.shape[3] // shares
    partial_spectra = transform(visibilities, m_order, "ma")
    got = lax.all_to_all(partial_spectra, "ma", split_axis=0, concat_axis=0, tiled=True)
    factor = factors(feed_pairs, feed_gains)
    partial_modes = project(got, factor, beam_blocks, shares)
    parts = lax.all_to_all(partial_modes, "bl", split_axis=0, concat_axis=0, tiled=True)
    return jnp.sum(parts, axis=0)[:, None, :share_width]


def solution(mesh):
    return jax.shard_map(
        per_device,
        mesh=mesh,
        in_specs=(P(None, "bl", "ma"), P("ma", None, "bl", None), P("bl", None), P(), P()),
        out_specs=P(None, "ma", "bl"),
        check_vma=False,
    )
```

```python
import jax
import jax.numpy as jnp
from jax import lax
from jax.experimental import pallas as pl
from jax.experimental.pallas import tpu as pltpu
from jax.sharding import PartitionSpec as P

NT = 8192
GROUPS = 4
EARLY = 3
LANES = 128
MIB = 1024 * 1024


def group_spans(rows):
    step = rows // GROUPS // LANES * LANES
    starts = [group * step for group in range(GROUPS)]
    return [(start, (starts[i + 1] if i + 1 < GROUPS else rows) - start) for i, start in enumerate(starts)]


def lane_pieces(size):
    return [(at, min(LANES, size - at)) for at in range(0, size, LANES)]


def padded(size):
    return -(-size // LANES) * LANES


def transform_kernel(spans, my_slot, m_ref, vis_ref, keep_ref, send_ref, held, lines, sems):
    copies = []
    for group, (start, size) in enumerate(spans):
        rows = pl.ds(start, size)
        copy = pltpu.make_async_copy(vis_ref.at[:, rows, :], held.at[:, rows, :], sems.at[group])
        copy.start()
        copies.append(copy)
    count = m_ref.shape[0]
    half = count // 2
    times = vis_ref.shape[2]
    parity = jnp.bitwise_and(my_slot, 1)
    row = lax.broadcasted_iota(jnp.int32, (count, LANES), 0)
    m_values = jnp.zeros((count, LANES), jnp.int32)
    for i in range(half):
        m_values = jnp.where(row == i, m_ref[2 * i + parity] - count // 2, m_values)
        m_values = jnp.where(row == half + i, m_ref[2 * i + 1 - parity] - count // 2, m_values)
    begin = my_slot * times
    scale = 1.0 / jnp.sqrt(jnp.float32(NT))
    cos_parts, sin_parts = [], []
    for at in range(0, times, LANES):
        t = begin + at + lax.broadcasted_iota(jnp.int32, (count, LANES), 1)
        wrapped = jnp.bitwise_and(t * m_values, NT - 1).astype(jnp.float32)
        phases = wrapped * (2.0 * jnp.pi / NT)
        cos_parts.append(jnp.cos(phases) * scale)
        sin_parts.append(jnp.sin(phases) * scale)
    cos_part = jnp.concatenate(cos_parts, axis=1)
    sin_part = jnp.concatenate(sin_parts, axis=1)
    for_real = jnp.concatenate([cos_part, -sin_part], axis=0).astype(jnp.bfloat16)
    for_imag = jnp.concatenate([sin_part, cos_part], axis=0).astype(jnp.bfloat16)
    contract = (((1,), (1,)), ((), ()))
    for group, (start, size) in enumerate(spans):
        copies[group].wait()
        rows = pl.ds(start, size)
        found = lax.dot_general(for_real, held[0, rows, :], contract, preferred_element_type=jnp.float32)
        found += lax.dot_general(for_imag, held[1, rows, :], contract, preferred_element_type=jnp.float32)
        for piece, (at, width) in enumerate(lane_pieces(lines.shape[0] * LANES)):
            for part in range(2):
                to = pl.ds(part * GROUPS + group, count, stride=2 * GROUPS)
                filled = min(width, max(size - at, 0))
                if filled < width:
                    lines[piece, to, :] = jnp.zeros((count, width), jnp.float32)
                if filled > 0:
                    lines[piece, to, :filled] = found[part * count:(part + 1) * count, at:at + filled]
    for piece in range(lines.shape[0]):
        block = lines[piece].reshape(count, 2 * GROUPS, LANES)
        keep_ref[:, :, piece * LANES:(piece + 1) * LANES] = block[:half]
        send_ref[:, :, piece * LANES:(piece + 1) * LANES] = block[half:]


def transform(visibilities, m_order, slot):
    rows, times = visibilities.shape[1:]
    count = m_order.shape[0]
    spans = group_spans(rows)
    width = padded(max(size for _, size in spans))

    def body(slot_ref, *refs):
        transform_kernel(spans, slot_ref[0], *refs)

    return pl.pallas_call(
        body,
        out_shape=[jax.ShapeDtypeStruct((count // 2, 2 * GROUPS, width), jnp.float32)] * 2,
        in_specs=[
            pl.BlockSpec(memory_space=pltpu.SMEM),
            pl.BlockSpec(memory_space=pltpu.SMEM),
            pl.BlockSpec(memory_space=pl.ANY),
        ],
        out_specs=[pl.BlockSpec(memory_space=pltpu.VMEM)] * 2,
        scratch_shapes=[
            pltpu.VMEM((2, rows, times), jnp.bfloat16),
            pltpu.VMEM((width // LANES, count * 2 * GROUPS, LANES), jnp.float32),
            pltpu.SemaphoreType.DMA((GROUPS,)),
        ],
        name="transform",
    )(slot.reshape(1), m_order, pltpu.with_memory_space_constraint(visibilities, pltpu.HBM))


def three_pieces(value):
    first = value.astype(jnp.bfloat16)
    rest = value - first.astype(jnp.float32)
    second = rest.astype(jnp.bfloat16)
    third = (rest - second.astype(jnp.float32)).astype(jnp.bfloat16)
    return [first, second, third]


def factor_kernel(spans, pairs_ref, gains_ref, beam_ref, out_ref, held_ref, sem):
    copy = pltpu.make_async_copy(beam_ref.at[0, 0, pl.ds(0, held_ref.shape[0]), :], held_ref, sem)
    copy.start()
    feeds = gains_ref.shape[1]
    tiles = feeds // LANES
    table = jnp.concatenate(
        [gains_ref[part:part + 1, tile * LANES:(tile + 1) * LANES] for part in range(2) for tile in range(tiles)], axis=0
    )
    pieces = jnp.concatenate(three_pieces(table), axis=0)
    tall = 2 * tiles
    out_ref[...] = jnp.zeros_like(out_ref)
    for group, (start, size) in enumerate(spans):
        picked = []
        for side in range(2):
            feed = pairs_ref[side:side + 1, pl.ds(start, size)]
            lane = jnp.bitwise_and(feed, LANES - 1)
            tile = lax.shift_right_logical(feed, LANES.bit_length() - 1)
            lane_iota = lax.broadcasted_iota(jnp.int32, (LANES, size), 0)
            one_hot = jnp.where(lane_iota == lane, 1.0, 0.0).astype(jnp.bfloat16)
            rows = jnp.dot(pieces, one_hot, preferred_element_type=jnp.float32)
            whole = (rows[:tall] + rows[tall:2 * tall]) + rows[2 * tall:]
            chosen = lax.broadcasted_iota(jnp.int32, (tiles, size), 0) == tile
            for part in range(2):
                picked.append(jnp.sum(jnp.where(chosen, whole[part * tiles:(part + 1) * tiles], 0.0), axis=0, keepdims=True))
        a_re, a_im, b_re, b_im = picked
        factor_re = a_re * b_re + a_im * b_im
        factor_im = a_im * b_re - a_re * b_im
        out_ref[0, group:group + 1, :size] = factor_re
        out_ref[0, GROUPS + group:GROUPS + group + 1, :size] = factor_re
        out_ref[1, group:group + 1, :size] = -factor_im
        out_ref[1, GROUPS + group:GROUPS + group + 1, :size] = factor_im
    copy.wait()


def factors(feed_pairs, feed_gains, beam_blocks):
    rows, width = beam_blocks.shape[2:]
    spans = group_spans(rows)
    line = padded(max(size for _, size in spans))

    def body(*refs):
        factor_kernel(spans, *refs)

    return pl.pallas_call(
        body,
        out_shape=[
            pltpu.VMEM((2, 2 * GROUPS, line), jnp.float32),
            pltpu.VMEM((spans[EARLY][0], width), jnp.bfloat16),
        ],
        in_specs=[
            pl.BlockSpec(memory_space=pltpu.VMEM),
            pl.BlockSpec(memory_space=pltpu.VMEM),
            pl.BlockSpec(memory_space=pltpu.HBM),
        ],
        out_specs=[pl.BlockSpec(memory_space=pltpu.VMEM)] * 2,
        scratch_shapes=[pltpu.SemaphoreType.DMA],
        cost_estimate=pl.CostEstimate(
            flops=2 * 2 * rows * 48 * 128, bytes_accessed=2 * spans[EARLY][0] * width + 8 * rows, transcendentals=0
        ),
        compiler_params=pltpu.CompilerParams(vmem_limit_bytes=16 * MIB),
        name="factors",
    )(jnp.transpose(feed_pairs), feed_gains, pltpu.with_memory_space_constraint(beam_blocks, pltpu.HBM))


def project_kernel(spans, shares, got_ref, factor_ref, early_ref, beam_ref, out_ref, held, sems):
    copies = {}
    for part in range(2):
        for group, (start, size) in enumerate(spans):
            if part == 0 and group < EARLY:
                continue
            rows = pl.ds(start, size)
            copies[part, group] = pltpu.make_async_copy(
                beam_ref.at[0, part, rows, :],
                held.at[pl.ds(part * spans[-1][1] + (start if part else 0), size), :],
                sems.at[part * GROUPS + group],
            )
            copies[part, group].start()
    total = got_ref[0].astype(jnp.float32)
    for source in range(1, got_ref.shape[0]):
        total += got_ref[source].astype(jnp.float32)
    swapped = jnp.concatenate([total[GROUPS:], total[:GROUPS]], axis=0)
    weighted = total * factor_ref[0] + swapped * factor_ref[1]
    high = weighted.astype(jnp.bfloat16)
    low = (weighted - high.astype(jnp.float32)).astype(jnp.bfloat16)
    rows16 = jnp.concatenate([high.astype(jnp.float32), low.astype(jnp.float32)], axis=0)
    row_group = jnp.bitwise_and(lax.broadcasted_iota(jnp.int32, rows16.shape, 0), GROUPS - 1)
    lefts = [jnp.where(row_group == group, rows16, 0.0).astype(jnp.bfloat16) for group in range(GROUPS)]
    sums = []
    for part in range(2):
        value = None
        for group, (start, size) in enumerate(spans):
            if (part, group) in copies:
                copies[part, group].wait()
                right = held[pl.ds(part * spans[-1][1] + (start if part else 0), size), :]
            else:
                right = early_ref[pl.ds(start, size), :]
            term = jnp.dot(lefts[group][:, :size], right, preferred_element_type=jnp.float32)
            value = term if value is None else value + term
        value = value[:2 * GROUPS] + value[2 * GROUPS:]
        sums.append(
            [jnp.sum(value[piece * GROUPS:(piece + 1) * GROUPS], axis=0, keepdims=True) for piece in range(2)]
        )
    answer = jnp.concatenate([sums[0][0] + sums[1][1], sums[0][1] - sums[1][0]], axis=0)
    width = answer.shape[1]
    share = width // shares
    for k in range(shares):
        out_ref[k, :, :share] = answer[:, k * share:(k + 1) * share]


def project(got, factor, early, beam_blocks, shares):
    rows, width = beam_blocks.shape[2:]
    spans = group_spans(rows)

    def body(*refs):
        project_kernel(spans, shares, *refs)

    return pl.pallas_call(
        body,
        out_shape=jax.ShapeDtypeStruct((shares, 2, padded(width // shares)), jnp.float32),
        in_specs=[pl.BlockSpec(memory_space=pltpu.VMEM)] * 3 + [pl.BlockSpec(memory_space=pltpu.HBM)],
        out_specs=pl.BlockSpec(memory_space=pltpu.VMEM),
        scratch_shapes=[
            pltpu.VMEM((spans[-1][1] + rows, width), jnp.bfloat16),
            pltpu.SemaphoreType.DMA((2 * GROUPS,)),
        ],
        compiler_params=pltpu.CompilerParams(vmem_limit_bytes=24 * MIB),
        name="project",
    )(
        *(pltpu.with_memory_space_constraint(held, pltpu.VMEM) for held in (got, factor, early)),
        pltpu.with_memory_space_constraint(beam_blocks, pltpu.HBM),
    )


def per_device(visibilities, beam_blocks, feed_pairs, feed_gains, m_order):
    shares = lax.axis_size("bl")
    slots = lax.axis_size("ma")
    share_width = beam_blocks.shape[3] // shares
    keep, send = transform(visibilities, m_order, lax.axis_index("ma"))
    other = lax.ppermute(send, "ma", [(slot, slot ^ 1) for slot in range(slots)])
    pair = (keep + other).astype(jnp.bfloat16)
    same_core = [[2 * i + parity for i in range(slots // 2)] for parity in range(2)]
    got = lax.all_to_all(pair, "ma", split_axis=0, concat_axis=0, tiled=True, axis_index_groups=same_core)
    factor, early = factors(feed_pairs, feed_gains, beam_blocks)
    partial_modes = project(got, factor, early, beam_blocks, shares)
    parts = lax.all_to_all(partial_modes, "bl", split_axis=0, concat_axis=0, tiled=True)
    return jnp.sum(parts, axis=0)[:, None, :share_width]


def solution(mesh):
    return jax.shard_map(
        per_device,
        mesh=mesh,
        in_specs=(P(None, "bl", "ma"), P("ma", None, "bl", None), P("bl", None), P(), P()),
        out_specs=P(None, "ma", "bl"),
        check_vma=False,
    )
```

```python
import jax
import jax.numpy as jnp
from jax import lax
from jax.experimental import pallas as pl
from jax.experimental.pallas import tpu as pltpu
from jax.sharding import PartitionSpec as P

NT = 8192
GROUPS = 4
EARLY = 3
LANES = 128
MIB = 1024 * 1024


def group_spans(rows):
    step = rows // GROUPS // LANES * LANES
    starts = [group * step for group in range(GROUPS)]
    return [(start, (starts[i + 1] if i + 1 < GROUPS else rows) - start) for i, start in enumerate(starts)]


def rotated(count, first):
    return [(first + i) % count for i in range(count)]


def lane_pieces(size):
    return [(at, min(LANES, size - at)) for at in range(0, size, LANES)]


def padded(size):
    return -(-size // LANES) * LANES


def transform_kernel(spans, order, my_slot, m_ref, vis_ref, keep_ref, send_ref, held, lines, sems):
    copies = []
    for group, (start, size) in enumerate(spans):
        rows = pl.ds(start, size)
        copy = pltpu.make_async_copy(vis_ref.at[:, rows, :], held.at[:, rows, :], sems.at[group])
        copy.start()
        copies.append(copy)
    count = m_ref.shape[0]
    half = count // 2
    times = vis_ref.shape[2]
    parity = jnp.bitwise_and(my_slot, 1)
    row = lax.broadcasted_iota(jnp.int32, (count, LANES), 0)
    m_values = jnp.zeros((count, LANES), jnp.int32)
    for i in range(half):
        m_values = jnp.where(row == i, m_ref[2 * order[i] + parity] - count // 2, m_values)
        m_values = jnp.where(row == half + i, m_ref[2 * order[i] + 1 - parity] - count // 2, m_values)
    begin = my_slot * times
    scale = 1.0 / jnp.sqrt(jnp.float32(NT))
    cos_parts, sin_parts = [], []
    for at in range(0, times, LANES):
        t = begin + at + lax.broadcasted_iota(jnp.int32, (count, LANES), 1)
        wrapped = jnp.bitwise_and(t * m_values, NT - 1).astype(jnp.float32)
        phases = wrapped * (2.0 * jnp.pi / NT)
        cos_parts.append(jnp.cos(phases) * scale)
        sin_parts.append(jnp.sin(phases) * scale)
    cos_part = jnp.concatenate(cos_parts, axis=1)
    sin_part = jnp.concatenate(sin_parts, axis=1)
    for_real = jnp.concatenate([cos_part, -sin_part], axis=0).astype(jnp.bfloat16)
    for_imag = jnp.concatenate([sin_part, cos_part], axis=0).astype(jnp.bfloat16)
    contract = (((1,), (1,)), ((), ()))
    for group, (start, size) in enumerate(spans):
        copies[group].wait()
        rows = pl.ds(start, size)
        found = lax.dot_general(for_real, held[0, rows, :], contract, preferred_element_type=jnp.float32)
        found += lax.dot_general(for_imag, held[1, rows, :], contract, preferred_element_type=jnp.float32)
        for piece, (at, width) in enumerate(lane_pieces(lines.shape[0] * LANES)):
            for part in range(2):
                to = pl.ds(part * GROUPS + group, count, stride=2 * GROUPS)
                filled = min(width, max(size - at, 0))
                if filled < width:
                    lines[piece, to, :] = jnp.zeros((count, width), jnp.float32)
                if filled > 0:
                    lines[piece, to, :filled] = found[part * count:(part + 1) * count, at:at + filled]
    for piece in range(lines.shape[0]):
        block = lines[piece].reshape(count, 2 * GROUPS, LANES)
        keep_ref[:, :, piece * LANES:(piece + 1) * LANES] = block[:half]
        send_ref[:, :, piece * LANES:(piece + 1) * LANES] = block[half:]


def transform(visibilities, m_order, slot, order):
    rows, times = visibilities.shape[1:]
    count = m_order.shape[0]
    spans = group_spans(rows)
    width = padded(max(size for _, size in spans))

    def body(slot_ref, *refs):
        transform_kernel(spans, order, slot_ref[0], *refs)

    return pl.pallas_call(
        body,
        out_shape=[pltpu.VMEM((count // 2, 2 * GROUPS, width), jnp.float32)] * 2,
        in_specs=[
            pl.BlockSpec(memory_space=pltpu.SMEM),
            pl.BlockSpec(memory_space=pltpu.SMEM),
            pl.BlockSpec(memory_space=pl.ANY),
        ],
        out_specs=[pl.BlockSpec(memory_space=pltpu.VMEM)] * 2,
        scratch_shapes=[
            pltpu.VMEM((2, rows, times), jnp.bfloat16),
            pltpu.VMEM((width // LANES, count * 2 * GROUPS, LANES), jnp.float32),
            pltpu.SemaphoreType.DMA((GROUPS,)),
        ],
        name="transform",
    )(slot.reshape(1), m_order, pltpu.with_memory_space_constraint(visibilities, pltpu.HBM))


def three_pieces(value):
    first = value.astype(jnp.bfloat16)
    rest = value - first.astype(jnp.float32)
    second = rest.astype(jnp.bfloat16)
    third = (rest - second.astype(jnp.float32)).astype(jnp.bfloat16)
    return [first, second, third]


def factor_kernel(spans, pairs_ref, gains_ref, beam_ref, out_ref, held_ref, sem):
    copy = pltpu.make_async_copy(beam_ref.at[0, 0, pl.ds(0, held_ref.shape[0]), :], held_ref, sem)
    copy.start()
    feeds = gains_ref.shape[1]
    tiles = feeds // LANES
    table = jnp.concatenate(
        [gains_ref[part:part + 1, tile * LANES:(tile + 1) * LANES] for part in range(2) for tile in range(tiles)], axis=0
    )
    pieces = jnp.concatenate(three_pieces(table), axis=0)
    tall = 2 * tiles
    out_ref[...] = jnp.zeros_like(out_ref)
    for group, (start, size) in enumerate(spans):
        picked = []
        for side in range(2):
            feed = pairs_ref[side:side + 1, pl.ds(start, size)]
            lane = jnp.bitwise_and(feed, LANES - 1)
            tile = lax.shift_right_logical(feed, LANES.bit_length() - 1)
            lane_iota = lax.broadcasted_iota(jnp.int32, (LANES, size), 0)
            one_hot = jnp.where(lane_iota == lane, 1.0, 0.0).astype(jnp.bfloat16)
            rows = jnp.dot(pieces, one_hot, preferred_element_type=jnp.float32)
            whole = (rows[:tall] + rows[tall:2 * tall]) + rows[2 * tall:]
            chosen = lax.broadcasted_iota(jnp.int32, (tiles, size), 0) == tile
            for part in range(2):
                picked.append(jnp.sum(jnp.where(chosen, whole[part * tiles:(part + 1) * tiles], 0.0), axis=0, keepdims=True))
        a_re, a_im, b_re, b_im = picked
        factor_re = a_re * b_re + a_im * b_im
        factor_im = a_im * b_re - a_re * b_im
        out_ref[0, group:group + 1, :size] = factor_re
        out_ref[0, GROUPS + group:GROUPS + group + 1, :size] = factor_re
        out_ref[1, group:group + 1, :size] = -factor_im
        out_ref[1, GROUPS + group:GROUPS + group + 1, :size] = factor_im
    copy.wait()


def factors(feed_pairs, feed_gains, beam_blocks):
    rows, width = beam_blocks.shape[2:]
    spans = group_spans(rows)
    line = padded(max(size for _, size in spans))

    def body(*refs):
        factor_kernel(spans, *refs)

    return pl.pallas_call(
        body,
        out_shape=[
            pltpu.VMEM((2, 2 * GROUPS, line), jnp.float32),
            pltpu.VMEM((spans[EARLY][0], width), jnp.bfloat16),
        ],
        in_specs=[
            pl.BlockSpec(memory_space=pltpu.VMEM),
            pl.BlockSpec(memory_space=pltpu.VMEM),
            pl.BlockSpec(memory_space=pltpu.HBM),
        ],
        out_specs=[pl.BlockSpec(memory_space=pltpu.VMEM)] * 2,
        scratch_shapes=[pltpu.SemaphoreType.DMA],
        cost_estimate=pl.CostEstimate(
            flops=2 * 2 * rows * 48 * 128, bytes_accessed=2 * spans[EARLY][0] * width + 8 * rows, transcendentals=0
        ),
        compiler_params=pltpu.CompilerParams(vmem_limit_bytes=16 * MIB),
        name="factors",
    )(jnp.transpose(feed_pairs), feed_gains, pltpu.with_memory_space_constraint(beam_blocks, pltpu.HBM))


def project_kernel(spans, share_order, got_ref, factor_ref, early_ref, beam_ref, out_ref, held, sems):
    copies = {}
    for part in range(2):
        for group, (start, size) in enumerate(spans):
            if part == 0 and group < EARLY:
                continue
            rows = pl.ds(start, size)
            copies[part, group] = pltpu.make_async_copy(
                beam_ref.at[0, part, rows, :],
                held.at[pl.ds(part * spans[-1][1] + (start if part else 0), size), :],
                sems.at[part * GROUPS + group],
            )
            copies[part, group].start()
    total = got_ref[0].astype(jnp.float32)
    for source in range(1, got_ref.shape[0]):
        total += got_ref[source].astype(jnp.float32)
    swapped = jnp.concatenate([total[GROUPS:], total[:GROUPS]], axis=0)
    weighted = total * factor_ref[0] + swapped * factor_ref[1]
    high = weighted.astype(jnp.bfloat16)
    low = (weighted - high.astype(jnp.float32)).astype(jnp.bfloat16)
    rows16 = jnp.concatenate([high.astype(jnp.float32), low.astype(jnp.float32)], axis=0)
    row_group = jnp.bitwise_and(lax.broadcasted_iota(jnp.int32, rows16.shape, 0), GROUPS - 1)
    lefts = [jnp.where(row_group == group, rows16, 0.0).astype(jnp.bfloat16) for group in range(GROUPS)]
    sums = []
    for part in range(2):
        value = None
        for group, (start, size) in enumerate(spans):
            if (part, group) in copies:
                copies[part, group].wait()
                right = held[pl.ds(part * spans[-1][1] + (start if part else 0), size), :]
            else:
                right = early_ref[pl.ds(start, size), :]
            term = jnp.dot(lefts[group][:, :size], right, preferred_element_type=jnp.float32)
            value = term if value is None else value + term
        value = value[:2 * GROUPS] + value[2 * GROUPS:]
        sums.append(
            [jnp.sum(value[piece * GROUPS:(piece + 1) * GROUPS], axis=0, keepdims=True) for piece in range(2)]
        )
    answer = jnp.concatenate([sums[0][0] + sums[1][1], sums[0][1] - sums[1][0]], axis=0)
    width = answer.shape[1]
    share = width // len(share_order)
    for slab, k in enumerate(share_order):
        out_ref[slab, :, :share] = answer[:, k * share:(k + 1) * share]


def project(got, factor, early, beam_blocks, share_order):
    rows, width = beam_blocks.shape[2:]
    spans = group_spans(rows)

    def body(*refs):
        project_kernel(spans, share_order, *refs)

    return pl.pallas_call(
        body,
        out_shape=jax.ShapeDtypeStruct((len(share_order), 2, padded(width // len(share_order))), jnp.float32),
        in_specs=[pl.BlockSpec(memory_space=pltpu.VMEM)] * 3 + [pl.BlockSpec(memory_space=pltpu.HBM)],
        out_specs=pl.BlockSpec(memory_space=pltpu.VMEM),
        scratch_shapes=[
            pltpu.VMEM((spans[-1][1] + rows, width), jnp.bfloat16),
            pltpu.SemaphoreType.DMA((2 * GROUPS,)),
        ],
        compiler_params=pltpu.CompilerParams(vmem_limit_bytes=24 * MIB),
        name="project",
    )(
        *(pltpu.with_memory_space_constraint(held, pltpu.VMEM) for held in (got, factor, early)),
        pltpu.with_memory_space_constraint(beam_blocks, pltpu.HBM),
    )


def per_device(visibilities, beam_blocks, feed_pairs, feed_gains, m_order):
    shares = lax.axis_size("bl")
    slots = lax.axis_size("ma")
    share_width = beam_blocks.shape[3] // shares
    order = rotated(slots // 2, slots // 4)
    keep, send = transform(visibilities, m_order, lax.axis_index("ma"), order)
    other = lax.ppermute(send, "ma", [(slot, slot ^ 1) for slot in range(slots)])
    pair = (keep + other).astype(jnp.bfloat16)
    same_core = [[2 * i + parity for i in order] for parity in range(2)]
    got = lax.all_to_all(pair, "ma", split_axis=0, concat_axis=0, tiled=True, axis_index_groups=same_core)
    factor, early = factors(feed_pairs, feed_gains, beam_blocks)
    share_order = rotated(shares, shares // 2 + 1)
    partial_modes = project(got, factor, early, beam_blocks, share_order)
    parts = lax.all_to_all(
        partial_modes, "bl", split_axis=0, concat_axis=0, tiled=True, axis_index_groups=[share_order]
    )
    return jnp.sum(parts, axis=0)[:, None, :share_width]


def solution(mesh):
    return jax.shard_map(
        per_device,
        mesh=mesh,
        in_specs=(P(None, "bl", "ma"), P("ma", None, "bl", None), P("bl", None), P(), P()),
        out_specs=P(None, "ma", "bl"),
        check_vma=False,
    )
```

```python
import jax
import jax.numpy as jnp
from jax import lax
from jax.experimental import pallas as pl
from jax.experimental.pallas import tpu as pltpu
from jax.sharding import PartitionSpec as P

NT = 8192
GROUPS = 4
LANES = 128
MIB = 1024 * 1024
FIRST_ROWS = 2080
SECOND_ROWS = 1536


def group_spans(rows):
    step = rows // GROUPS // LANES * LANES
    starts = [group * step for group in range(GROUPS)]
    return [(start, (starts[i + 1] if i + 1 < GROUPS else rows) - start) for i, start in enumerate(starts)]


def rotated(count, first):
    return [(first + i) % count for i in range(count)]


def lane_pieces(size):
    return [(at, min(LANES, size - at)) for at in range(0, size, LANES)]


def padded(size):
    return -(-size // LANES) * LANES


def transform_kernel(
    spans, order, my_slot, given_m, vis_ref, beam_ref, keep_ref, send_ref, early_ref, held, lines, m_ref, sems
):
    fetch_m = pltpu.make_async_copy(given_m, m_ref, sems.at[GROUPS + 1])
    fetch_m.start()
    copies = []
    for group, (start, size) in enumerate(spans):
        rows = pl.ds(start, size)
        copy = pltpu.make_async_copy(vis_ref.at[:, rows, :], held.at[:, rows, :], sems.at[group])
        copy.start()
        copies.append(copy)
    early = pltpu.make_async_copy(beam_ref.at[pl.ds(0, early_ref.shape[0]), :], early_ref, sems.at[GROUPS])
    early.start()
    fetch_m.wait()
    count = m_ref.shape[0]
    half = count // 2
    times = vis_ref.shape[2]
    parity = jnp.bitwise_and(my_slot, 1)
    row = lax.broadcasted_iota(jnp.int32, (count, LANES), 0)
    m_values = jnp.zeros((count, LANES), jnp.int32)
    for i in range(half):
        m_values = jnp.where(row == i, m_ref[2 * order[i] + parity] - count // 2, m_values)
        m_values = jnp.where(row == half + i, m_ref[2 * order[i] + 1 - parity] - count // 2, m_values)
    begin = my_slot * times
    scale = 1.0 / jnp.sqrt(jnp.float32(NT))
    cos_parts, sin_parts = [], []
    for at in range(0, times, LANES):
        t = begin + at + lax.broadcasted_iota(jnp.int32, (count, LANES), 1)
        wrapped = jnp.bitwise_and(t * m_values, NT - 1).astype(jnp.float32)
        phases = wrapped * (2.0 * jnp.pi / NT)
        cos_parts.append(jnp.cos(phases) * scale)
        sin_parts.append(jnp.sin(phases) * scale)
    cos_part = jnp.concatenate(cos_parts, axis=1)
    sin_part = jnp.concatenate(sin_parts, axis=1)
    for_real = jnp.concatenate([cos_part, -sin_part], axis=0).astype(jnp.bfloat16)
    for_imag = jnp.concatenate([sin_part, cos_part], axis=0).astype(jnp.bfloat16)
    contract = (((1,), (1,)), ((), ()))
    for group, (start, size) in enumerate(spans):
        copies[group].wait()
        rows = pl.ds(start, size)
        found = lax.dot_general(for_real, held[0, rows, :], contract, preferred_element_type=jnp.float32)
        found += lax.dot_general(for_imag, held[1, rows, :], contract, preferred_element_type=jnp.float32)
        for piece, (at, width) in enumerate(lane_pieces(lines.shape[0] * LANES)):
            for part in range(2):
                to = pl.ds(part * GROUPS + group, count, stride=2 * GROUPS)
                filled = min(width, max(size - at, 0))
                if filled < width:
                    lines[piece, to, :] = jnp.zeros((count, width), jnp.float32)
                if filled > 0:
                    lines[piece, to, :filled] = found[part * count:(part + 1) * count, at:at + filled]
    for piece in range(lines.shape[0]):
        block = lines[piece].reshape(count, 2 * GROUPS, LANES)
        keep_ref[:, :, piece * LANES:(piece + 1) * LANES] = block[:half]
        send_ref[:, :, piece * LANES:(piece + 1) * LANES] = block[half:]
    early.wait()


def transform(visibilities, beam, m_order, slot, order):
    rows, times = visibilities.shape[1:]
    count = m_order.shape[0]
    spans = group_spans(rows)
    width = padded(max(size for _, size in spans))

    def body(slot_ref, *refs):
        transform_kernel(spans, order, slot_ref[0], *refs)

    return pl.pallas_call(
        body,
        out_shape=[pltpu.VMEM((count // 2, 2 * GROUPS, width), jnp.float32)] * 2
        + [pltpu.VMEM((FIRST_ROWS, beam.shape[1]), jnp.bfloat16)],
        in_specs=[
            pl.BlockSpec(memory_space=pltpu.SMEM),
            pl.BlockSpec(memory_space=pltpu.HBM),
            pl.BlockSpec(memory_space=pltpu.HBM),
            pl.BlockSpec(memory_space=pltpu.HBM),
        ],
        out_specs=[pl.BlockSpec(memory_space=pltpu.VMEM)] * 3,
        scratch_shapes=[
            pltpu.VMEM((2, rows, times), jnp.bfloat16),
            pltpu.VMEM((width // LANES, count * 2 * GROUPS, LANES), jnp.float32),
            pltpu.SMEM((count,), jnp.int32),
            pltpu.SemaphoreType.DMA((GROUPS + 2,)),
        ],
        compiler_params=pltpu.CompilerParams(vmem_limit_bytes=24 * MIB),
        name="transform",
    )(
        slot.reshape(1),
        *(pltpu.with_memory_space_constraint(given, pltpu.HBM) for given in (m_order, visibilities, beam)),
    )


def three_pieces(value):
    first = value.astype(jnp.bfloat16)
    rest = value - first.astype(jnp.float32)
    second = rest.astype(jnp.bfloat16)
    third = (rest - second.astype(jnp.float32)).astype(jnp.bfloat16)
    return [first, second, third]


def factor_kernel(spans, given_pairs, given_gains, beam_ref, out_ref, early_ref, pairs_ref, gains_ref, sems):
    fetches = [
        pltpu.make_async_copy(given_pairs, pairs_ref, sems.at[0]),
        pltpu.make_async_copy(given_gains, gains_ref, sems.at[1]),
        pltpu.make_async_copy(beam_ref.at[pl.ds(FIRST_ROWS, early_ref.shape[0]), :], early_ref, sems.at[2]),
    ]
    for fetch in fetches:
        fetch.start()
    for fetch in fetches[:2]:
        fetch.wait()
    feeds = gains_ref.shape[1]
    tiles = feeds // LANES
    table = jnp.concatenate(
        [gains_ref[part:part + 1, tile * LANES:(tile + 1) * LANES] for part in range(2) for tile in range(tiles)], axis=0
    )
    pieces = jnp.concatenate(three_pieces(table), axis=0)
    tall = 2 * tiles
    out_ref[...] = jnp.zeros_like(out_ref)
    for group, (start, size) in enumerate(spans):
        picked = []
        for side in range(2):
            feed = pairs_ref[side:side + 1, pl.ds(start, size)]
            lane = jnp.bitwise_and(feed, LANES - 1)
            tile = lax.shift_right_logical(feed, LANES.bit_length() - 1)
            lane_iota = lax.broadcasted_iota(jnp.int32, (LANES, size), 0)
            one_hot = jnp.where(lane_iota == lane, 1.0, 0.0).astype(jnp.bfloat16)
            rows = jnp.dot(pieces, one_hot, preferred_element_type=jnp.float32)
            whole = (rows[:tall] + rows[tall:2 * tall]) + rows[2 * tall:]
            chosen = lax.broadcasted_iota(jnp.int32, (tiles, size), 0) == tile
            for part in range(2):
                picked.append(jnp.sum(jnp.where(chosen, whole[part * tiles:(part + 1) * tiles], 0.0), axis=0, keepdims=True))
        a_re, a_im, b_re, b_im = picked
        factor_re = a_re * b_re + a_im * b_im
        factor_im = a_im * b_re - a_re * b_im
        out_ref[0, group:group + 1, :size] = factor_re
        out_ref[0, GROUPS + group:GROUPS + group + 1, :size] = factor_re
        out_ref[1, group:group + 1, :size] = -factor_im
        out_ref[1, GROUPS + group:GROUPS + group + 1, :size] = factor_im
    fetches[2].wait()


def factors(feed_pairs, feed_gains, beam):
    rows, width = feed_pairs.shape[0], beam.shape[1]
    spans = group_spans(rows)
    line = padded(max(size for _, size in spans))

    def body(*refs):
        factor_kernel(spans, *refs)

    return pl.pallas_call(
        body,
        out_shape=[
            pltpu.VMEM((2, 2 * GROUPS, line), jnp.float32),
            pltpu.VMEM((SECOND_ROWS, width), jnp.bfloat16),
        ],
        in_specs=[pl.BlockSpec(memory_space=pltpu.HBM)] * 3,
        out_specs=[pl.BlockSpec(memory_space=pltpu.VMEM)] * 2,
        scratch_shapes=[
            pltpu.VMEM(feed_pairs.shape[::-1], jnp.int32),
            pltpu.VMEM(feed_gains.shape, jnp.float32),
            pltpu.SemaphoreType.DMA((3,)),
        ],
        cost_estimate=pl.CostEstimate(
            flops=2 * 2 * rows * 48 * 128, bytes_accessed=2 * SECOND_ROWS * width + 8 * rows, transcendentals=0
        ),
        compiler_params=pltpu.CompilerParams(vmem_limit_bytes=16 * MIB),
        name="factors",
    )(
        *(
            pltpu.with_memory_space_constraint(given, pltpu.HBM)
            for given in (jnp.transpose(feed_pairs), feed_gains, beam)
        )
    )


def project_kernel(spans, share_order, got_ref, factor_ref, first_ref, second_ref, beam_ref, out_ref, last_ref, sem):
    places = []
    begin = 0
    for ref in (first_ref, second_ref, last_ref):
        places.append((begin, ref))
        begin += ref.shape[0]
    late = pltpu.make_async_copy(beam_ref.at[pl.ds(places[-1][0], last_ref.shape[0]), :], last_ref, sem)
    late.start()
    total = got_ref[0].astype(jnp.float32)
    for source in range(1, got_ref.shape[0]):
        total += got_ref[source].astype(jnp.float32)
    swapped = jnp.concatenate([total[GROUPS:], total[:GROUPS]], axis=0)
    weighted = total * factor_ref[0] + swapped * factor_ref[1]
    high = weighted.astype(jnp.bfloat16)
    low = (weighted - high.astype(jnp.float32)).astype(jnp.bfloat16)
    rows16 = jnp.concatenate([high.astype(jnp.float32), low.astype(jnp.float32)], axis=0)
    row_group = jnp.bitwise_and(lax.broadcasted_iota(jnp.int32, rows16.shape, 0), GROUPS - 1)
    lefts = [jnp.where(row_group == group, rows16, 0.0).astype(jnp.bfloat16) for group in range(GROUPS)]
    sums = []
    waited = False
    for part in range(2):
        value = None
        for group, (start, size) in enumerate(spans):
            row = part * (spans[-1][0] + spans[-1][1]) + start
            for begin, ref in places:
                low = max(row, begin)
                count = min(row + size, begin + ref.shape[0]) - low
                if count <= 0:
                    continue
                if ref is last_ref and not waited:
                    late.wait()
                    waited = True
                left = lefts[group][:, low - row:low - row + count]
                term = jnp.dot(left, ref[pl.ds(low - begin, count), :], preferred_element_type=jnp.float32)
                value = term if value is None else value + term
        value = value[:2 * GROUPS] + value[2 * GROUPS:]
        sums.append(
            [jnp.sum(value[piece * GROUPS:(piece + 1) * GROUPS], axis=0, keepdims=True) for piece in range(2)]
        )
    answer = jnp.concatenate([sums[0][0] + sums[1][1], sums[0][1] - sums[1][0]], axis=0)
    width = answer.shape[1]
    share = width // len(share_order)
    for slab, k in enumerate(share_order):
        out_ref[slab, :, :share] = answer[:, k * share:(k + 1) * share]


def project(got, factor, first, second, beam, share_order):
    rows, width = beam.shape
    spans = group_spans(rows // 2)

    def body(*refs):
        project_kernel(spans, share_order, *refs)

    return pl.pallas_call(
        body,
        out_shape=jax.ShapeDtypeStruct((len(share_order), 2, padded(width // len(share_order))), jnp.float32),
        in_specs=[pl.BlockSpec(memory_space=pltpu.VMEM)] * 4 + [pl.BlockSpec(memory_space=pltpu.HBM)],
        out_specs=pl.BlockSpec(memory_space=pltpu.VMEM),
        scratch_shapes=[pltpu.VMEM((rows - FIRST_ROWS - SECOND_ROWS, width), jnp.bfloat16), pltpu.SemaphoreType.DMA],
        compiler_params=pltpu.CompilerParams(vmem_limit_bytes=16 * MIB),
        name="project",
    )(
        *(pltpu.with_memory_space_constraint(held, pltpu.VMEM) for held in (got, factor, first, second)),
        pltpu.with_memory_space_constraint(beam, pltpu.HBM),
    )


def per_device(visibilities, beam_blocks, feed_pairs, feed_gains, m_order):
    shares = lax.axis_size("bl")
    slots = lax.axis_size("ma")
    share_width = beam_blocks.shape[3] // shares
    order = rotated(slots // 2, slots // 4)
    beam = beam_blocks.reshape(2 * beam_blocks.shape[2], beam_blocks.shape[3])
    keep, send, first = transform(visibilities, beam, m_order, lax.axis_index("ma"), order)
    send, feed_gains = lax.optimization_barrier((send, feed_gains))
    factor, second = factors(feed_pairs, feed_gains, beam)
    other = lax.ppermute(send, "ma", [(slot, slot ^ 1) for slot in range(slots)])
    pair, factor = lax.optimization_barrier(((keep + other).astype(jnp.bfloat16), factor))
    same_core = [[2 * i + parity for i in order] for parity in range(2)]
    got = lax.all_to_all(pair, "ma", split_axis=0, concat_axis=0, tiled=True, axis_index_groups=same_core)
    share_order = rotated(shares, shares // 2 + 1)
    partial_modes = project(got, factor, first, second, beam, share_order)
    parts = lax.all_to_all(
        partial_modes, "bl", split_axis=0, concat_axis=0, tiled=True, axis_index_groups=[share_order]
    )
    return jnp.sum(parts, axis=0)[:, None, :share_width]


def solution(mesh):
    return jax.shard_map(
        per_device,
        mesh=mesh,
        in_specs=(P(None, "bl", "ma"), P("ma", None, "bl", None), P("bl", None), P(), P()),
        out_specs=P(None, "ma", "bl"),
        check_vma=False,
    )
```

```python
import jax
import jax.numpy as jnp
from jax import lax
from jax.experimental import pallas as pl
from jax.experimental.pallas import tpu as pltpu
from jax.sharding import PartitionSpec as P

NT = 8192
GROUPS = 4
LANES = 128
MIB = 1024 * 1024


def group_spans(rows):
    step = rows // GROUPS // LANES * LANES
    starts = [group * step for group in range(GROUPS)]
    return [(start, (starts[i + 1] if i + 1 < GROUPS else rows) - start) for i, start in enumerate(starts)]


def rotated(count, first):
    return [(first + i) % count for i in range(count)]


def lane_pieces(size):
    return [(at, min(LANES, size - at)) for at in range(0, size, LANES)]


def padded(size):
    return -(-size // LANES) * LANES


def transform_kernel(
    spans, order, my_slot, given_m, vis_ref, beam_ref, keep_ref, send_ref, early_ref, held, lines, m_ref, sems
):
    fetch_m = pltpu.make_async_copy(given_m, m_ref, sems.at[GROUPS + 1])
    fetch_m.start()
    copies = []
    for group, (start, size) in enumerate(spans):
        rows = pl.ds(start, size)
        copy = pltpu.make_async_copy(vis_ref.at[:, rows, :], held.at[:, rows, :], sems.at[group])
        copy.start()
        copies.append(copy)
    early = pltpu.make_async_copy(beam_ref.at[pl.ds(0, early_ref.shape[0]), :], early_ref, sems.at[GROUPS])
    early.start()
    fetch_m.wait()
    count = m_ref.shape[0]
    half = count // 2
    times = vis_ref.shape[2]
    parity = jnp.bitwise_and(my_slot, 1)
    row = lax.broadcasted_iota(jnp.int32, (count, LANES), 0)
    m_values = jnp.zeros((count, LANES), jnp.int32)
    for i in range(half):
        m_values = jnp.where(row == i, m_ref[2 * order[i] + parity] - count // 2, m_values)
        m_values = jnp.where(row == half + i, m_ref[2 * order[i] + 1 - parity] - count // 2, m_values)
    begin = my_slot * times
    scale = 1.0 / jnp.sqrt(jnp.float32(NT))
    cos_parts, sin_parts = [], []
    for at in range(0, times, LANES):
        t = begin + at + lax.broadcasted_iota(jnp.int32, (count, LANES), 1)
        wrapped = jnp.bitwise_and(t * m_values, NT - 1).astype(jnp.float32)
        phases = wrapped * (2.0 * jnp.pi / NT)
        cos_parts.append(jnp.cos(phases) * scale)
        sin_parts.append(jnp.sin(phases) * scale)
    cos_part = jnp.concatenate(cos_parts, axis=1)
    sin_part = jnp.concatenate(sin_parts, axis=1)
    for_real = jnp.concatenate([cos_part, -sin_part], axis=0).astype(jnp.bfloat16)
    for_imag = jnp.concatenate([sin_part, cos_part], axis=0).astype(jnp.bfloat16)
    contract = (((1,), (1,)), ((), ()))
    for group, (start, size) in enumerate(spans):
        copies[group].wait()
        rows = pl.ds(start, size)
        found = lax.dot_general(for_real, held[0, rows, :], contract, preferred_element_type=jnp.float32)
        found += lax.dot_general(for_imag, held[1, rows, :], contract, preferred_element_type=jnp.float32)
        for piece, (at, width) in enumerate(lane_pieces(lines.shape[0] * LANES)):
            for part in range(2):
                to = pl.ds(part * GROUPS + group, count, stride=2 * GROUPS)
                filled = min(width, max(size - at, 0))
                if filled < width:
                    lines[piece, to, :] = jnp.zeros((count, width), jnp.float32)
                if filled > 0:
                    lines[piece, to, :filled] = found[part * count:(part + 1) * count, at:at + filled]
    for piece in range(lines.shape[0]):
        block = lines[piece].reshape(count, 2 * GROUPS, LANES)
        keep_ref[:, :, piece * LANES:(piece + 1) * LANES] = block[:half]
        send_ref[:, :, piece * LANES:(piece + 1) * LANES] = block[half:]
    early.wait()


def transform(visibilities, beam, m_order, slot, order):
    rows, times = visibilities.shape[1:]
    count = m_order.shape[0]
    spans = group_spans(rows)
    width = padded(max(size for _, size in spans))

    def body(slot_ref, *refs):
        transform_kernel(spans, order, slot_ref[0], *refs)

    return pl.pallas_call(
        body,
        out_shape=[pltpu.VMEM((count // 2, 2 * GROUPS, width), jnp.float32)] * 2
        + [pltpu.VMEM((beam.shape[0] // 2, beam.shape[1]), jnp.bfloat16)],
        in_specs=[
            pl.BlockSpec(memory_space=pltpu.SMEM),
            pl.BlockSpec(memory_space=pltpu.HBM),
            pl.BlockSpec(memory_space=pltpu.HBM),
            pl.BlockSpec(memory_space=pltpu.HBM),
        ],
        out_specs=[pl.BlockSpec(memory_space=pltpu.VMEM)] * 3,
        scratch_shapes=[
            pltpu.VMEM((2, rows, times), jnp.bfloat16),
            pltpu.VMEM((width // LANES, count * 2 * GROUPS, LANES), jnp.float32),
            pltpu.SMEM((count,), jnp.int32),
            pltpu.SemaphoreType.DMA((GROUPS + 2,)),
        ],
        compiler_params=pltpu.CompilerParams(vmem_limit_bytes=24 * MIB),
        name="transform",
    )(
        slot.reshape(1),
        *(pltpu.with_memory_space_constraint(given, pltpu.HBM) for given in (m_order, visibilities, beam)),
    )


def three_pieces(value):
    first = value.astype(jnp.bfloat16)
    rest = value - first.astype(jnp.float32)
    second = rest.astype(jnp.bfloat16)
    third = (rest - second.astype(jnp.float32)).astype(jnp.bfloat16)
    return [first, second, third]


def factor_kernel(
    spans, eager, given_pairs, given_gains, beam_ref, out_ref, early_ref, pairs_ref, gains_ref, sems
):
    fetches = [
        pltpu.make_async_copy(given_pairs, pairs_ref, sems.at[0]),
        pltpu.make_async_copy(given_gains, gains_ref, sems.at[1]),
    ]
    for fetch in fetches:
        fetch.start()
    early = pltpu.make_async_copy(beam_ref.at[pl.ds(early_ref.shape[0], early_ref.shape[0]), :], early_ref, sems.at[2])

    @pl.when(eager)
    def start_early():
        early.start()

    for fetch in fetches:
        fetch.wait()
    feeds = gains_ref.shape[1]
    tiles = feeds // LANES
    table = jnp.concatenate(
        [gains_ref[part:part + 1, tile * LANES:(tile + 1) * LANES] for part in range(2) for tile in range(tiles)], axis=0
    )
    pieces = jnp.concatenate(three_pieces(table), axis=0)
    tall = 2 * tiles
    out_ref[...] = jnp.zeros_like(out_ref)
    for group, (start, size) in enumerate(spans):
        picked = []
        for side in range(2):
            feed = pairs_ref[side:side + 1, pl.ds(start, size)]
            lane = jnp.bitwise_and(feed, LANES - 1)
            tile = lax.shift_right_logical(feed, LANES.bit_length() - 1)
            lane_iota = lax.broadcasted_iota(jnp.int32, (LANES, size), 0)
            one_hot = jnp.where(lane_iota == lane, 1.0, 0.0).astype(jnp.bfloat16)
            rows = jnp.dot(pieces, one_hot, preferred_element_type=jnp.float32)
            whole = (rows[:tall] + rows[tall:2 * tall]) + rows[2 * tall:]
            chosen = lax.broadcasted_iota(jnp.int32, (tiles, size), 0) == tile
            for part in range(2):
                picked.append(jnp.sum(jnp.where(chosen, whole[part * tiles:(part + 1) * tiles], 0.0), axis=0, keepdims=True))
        a_re, a_im, b_re, b_im = picked
        factor_re = a_re * b_re + a_im * b_im
        factor_im = a_im * b_re - a_re * b_im
        out_ref[0, group:group + 1, :size] = factor_re
        out_ref[0, GROUPS + group:GROUPS + group + 1, :size] = factor_re
        out_ref[1, group:group + 1, :size] = -factor_im
        out_ref[1, GROUPS + group:GROUPS + group + 1, :size] = factor_im

    @pl.when(eager)
    def finish_early():
        early.wait()


def factors(feed_pairs, feed_gains, beam, slot, eager_slots):
    rows, width = feed_pairs.shape[0], beam.shape[1]
    spans = group_spans(rows)
    line = padded(max(size for _, size in spans))

    def body(slot_ref, *refs):
        factor_kernel(spans, slot_ref[0] < eager_slots, *refs)

    return pl.pallas_call(
        body,
        out_shape=[
            pltpu.VMEM((2, 2 * GROUPS, line), jnp.float32),
            pltpu.VMEM((rows, width), jnp.bfloat16),
        ],
        in_specs=[pl.BlockSpec(memory_space=pltpu.SMEM)] + [pl.BlockSpec(memory_space=pltpu.HBM)] * 3,
        out_specs=[pl.BlockSpec(memory_space=pltpu.VMEM)] * 2,
        scratch_shapes=[
            pltpu.VMEM(feed_pairs.shape[::-1], jnp.int32),
            pltpu.VMEM(feed_gains.shape, jnp.float32),
            pltpu.SemaphoreType.DMA((3,)),
        ],
        cost_estimate=pl.CostEstimate(
            flops=2 * 2 * rows * 48 * 128, bytes_accessed=2 * rows * width + 8 * rows, transcendentals=0
        ),
        compiler_params=pltpu.CompilerParams(vmem_limit_bytes=16 * MIB),
        name="factors",
    )(
        slot.reshape(1),
        *(
            pltpu.with_memory_space_constraint(given, pltpu.HBM)
            for given in (jnp.transpose(feed_pairs), feed_gains, beam)
        ),
    )


def project_kernel(
    spans, share_order, eager, got_ref, factor_ref, first_ref, second_ref, beam_ref, out_ref, late_ref, partial, sems
):
    rows = first_ref.shape[0]
    late = [
        pltpu.make_async_copy(
            beam_ref.at[pl.ds(rows + start, size), :], late_ref.at[pl.ds(start, size), :], sems.at[group]
        )
        for group, (start, size) in enumerate(spans)
    ]

    @pl.when(jnp.logical_not(eager))
    def start_late():
        for copy in late:
            copy.start()

    total = got_ref[0].astype(jnp.float32)
    for source in range(1, got_ref.shape[0]):
        total += got_ref[source].astype(jnp.float32)
    swapped = jnp.concatenate([total[GROUPS:], total[:GROUPS]], axis=0)
    weighted = total * factor_ref[0] + swapped * factor_ref[1]
    high = weighted.astype(jnp.bfloat16)
    low = (weighted - high.astype(jnp.float32)).astype(jnp.bfloat16)
    rows16 = jnp.concatenate([high.astype(jnp.float32), low.astype(jnp.float32)], axis=0)
    row_group = jnp.bitwise_and(lax.broadcasted_iota(jnp.int32, rows16.shape, 0), GROUPS - 1)
    lefts = [jnp.where(row_group == group, rows16, 0.0).astype(jnp.bfloat16) for group in range(GROUPS)]

    def products(ref, copies):
        value = None
        for group, (start, size) in enumerate(spans):
            if copies:
                copies[group].wait()
            term = jnp.dot(
                lefts[group][:, :size], ref[pl.ds(start, size), :], preferred_element_type=jnp.float32
            )
            value = term if value is None else value + term
        return value

    def collected(value):
        value = value[:2 * GROUPS] + value[2 * GROUPS:]
        return [jnp.sum(value[piece * GROUPS:(piece + 1) * GROUPS], axis=0, keepdims=True) for piece in range(2)]

    sums = [collected(products(first_ref, None))]

    @pl.when(eager)
    def use_early():
        partial[...] = products(second_ref, None)

    @pl.when(jnp.logical_not(eager))
    def use_late():
        partial[...] = products(late_ref, late)

    sums.append(collected(partial[...]))
    answer = jnp.concatenate([sums[0][0] + sums[1][1], sums[0][1] - sums[1][0]], axis=0)
    width = answer.shape[1]
    share = width // len(share_order)
    for slab, k in enumerate(share_order):
        out_ref[slab, :, :share] = answer[:, k * share:(k + 1) * share]


def project(got, factor, first, second, beam, share_order, slot, eager_slots):
    rows, width = beam.shape
    spans = group_spans(rows // 2)

    def body(slot_ref, *refs):
        project_kernel(spans, share_order, slot_ref[0] < eager_slots, *refs)

    return pl.pallas_call(
        body,
        out_shape=jax.ShapeDtypeStruct((len(share_order), 2, padded(width // len(share_order))), jnp.float32),
        in_specs=[pl.BlockSpec(memory_space=pltpu.SMEM)]
        + [pl.BlockSpec(memory_space=pltpu.VMEM)] * 4
        + [pl.BlockSpec(memory_space=pltpu.HBM)],
        out_specs=pl.BlockSpec(memory_space=pltpu.VMEM),
        scratch_shapes=[
            pltpu.VMEM((rows // 2, width), jnp.bfloat16),
            pltpu.VMEM((4 * GROUPS, width), jnp.float32),
            pltpu.SemaphoreType.DMA((GROUPS,)),
        ],
        compiler_params=pltpu.CompilerParams(vmem_limit_bytes=16 * MIB),
        name="project",
    )(
        slot.reshape(1),
        *(pltpu.with_memory_space_constraint(held, pltpu.VMEM) for held in (got, factor, first, second)),
        pltpu.with_memory_space_constraint(beam, pltpu.HBM),
    )


def per_device(visibilities, beam_blocks, feed_pairs, feed_gains, m_order):
    shares = lax.axis_size("bl")
    slots = lax.axis_size("ma")
    share_width = beam_blocks.shape[3] // shares
    order = rotated(slots // 2, slots // 4)
    beam = beam_blocks.reshape(2 * beam_blocks.shape[2], beam_blocks.shape[3])
    slot = lax.axis_index("ma")
    keep, send, first = transform(visibilities, beam, m_order, slot, order)
    send, feed_gains = lax.optimization_barrier((send, feed_gains))
    factor, second = factors(feed_pairs, feed_gains, beam, slot, slots // 2)
    other = lax.ppermute(send, "ma", [(slot, slot ^ 1) for slot in range(slots)])
    pair, factor = lax.optimization_barrier(((keep + other).astype(jnp.bfloat16), factor))
    same_core = [[2 * i + parity for i in order] for parity in range(2)]
    got = lax.all_to_all(pair, "ma", split_axis=0, concat_axis=0, tiled=True, axis_index_groups=same_core)
    share_order = rotated(shares, shares // 2 + 1)
    partial_modes = project(got, factor, first, second, beam, share_order, slot, slots // 2)
    parts = lax.all_to_all(
        partial_modes, "bl", split_axis=0, concat_axis=0, tiled=True, axis_index_groups=[share_order]
    )
    return jnp.sum(parts, axis=0)[:, None, :share_width]


def solution(mesh):
    return jax.shard_map(
        per_device,
        mesh=mesh,
        in_specs=(P(None, "bl", "ma"), P("ma", None, "bl", None), P("bl", None), P(), P()),
        out_specs=P(None, "ma", "bl"),
        check_vma=False,
    )
```

```python
import jax
import jax.numpy as jnp
from jax import lax
from jax.experimental import pallas as pl
from jax.experimental.pallas import tpu as pltpu
from jax.sharding import PartitionSpec as P

NT = 8192
GROUPS = 4
LANES = 128
MIB = 1024 * 1024


def group_spans(rows):
    step = rows // GROUPS // LANES * LANES
    starts = [group * step for group in range(GROUPS)]
    return [(start, (starts[i + 1] if i + 1 < GROUPS else rows) - start) for i, start in enumerate(starts)]


def rotated(count, first):
    return [(first + i) % count for i in range(count)]


def lane_pieces(size):
    return [(at, min(LANES, size - at)) for at in range(0, size, LANES)]


def padded(size):
    return -(-size // LANES) * LANES


def transform_kernel(
    spans, order, my_slot, given_m, vis_ref, beam_ref, keep_ref, send_ref, early_ref, held, lines, m_ref, sems
):
    fetch_m = pltpu.make_async_copy(given_m, m_ref, sems.at[GROUPS + 1])
    fetch_m.start()
    copies = []
    for group, (start, size) in enumerate(spans):
        rows = pl.ds(start, size)
        copy = pltpu.make_async_copy(vis_ref.at[:, rows, :], held.at[:, rows, :], sems.at[group])
        copy.start()
        copies.append(copy)
    early = pltpu.make_async_copy(beam_ref.at[pl.ds(0, early_ref.shape[0]), :], early_ref, sems.at[GROUPS])
    early.start()
    fetch_m.wait()
    count = m_ref.shape[0]
    half = count // 2
    times = vis_ref.shape[2]
    parity = jnp.bitwise_and(my_slot, 1)
    row = lax.broadcasted_iota(jnp.int32, (count, LANES), 0)
    m_values = jnp.zeros((count, LANES), jnp.int32)
    for i in range(half):
        m_values = jnp.where(row == i, m_ref[2 * order[i] + parity] - count // 2, m_values)
        m_values = jnp.where(row == half + i, m_ref[2 * order[i] + 1 - parity] - count // 2, m_values)
    begin = my_slot * times
    scale = 1.0 / jnp.sqrt(jnp.float32(NT))
    cos_parts, sin_parts = [], []
    for at in range(0, times, LANES):
        t = begin + at + lax.broadcasted_iota(jnp.int32, (count, LANES), 1)
        wrapped = jnp.bitwise_and(t * m_values, NT - 1).astype(jnp.float32)
        phases = wrapped * (2.0 * jnp.pi / NT)
        cos_parts.append(jnp.cos(phases) * scale)
        sin_parts.append(jnp.sin(phases) * scale)
    cos_part = jnp.concatenate(cos_parts, axis=1)
    sin_part = jnp.concatenate(sin_parts, axis=1)
    for_real = jnp.concatenate([cos_part, -sin_part], axis=0).astype(jnp.bfloat16)
    for_imag = jnp.concatenate([sin_part, cos_part], axis=0).astype(jnp.bfloat16)
    contract = (((1,), (1,)), ((), ()))
    for group, (start, size) in enumerate(spans):
        copies[group].wait()
        rows = pl.ds(start, size)
        found = lax.dot_general(for_real, held[0, rows, :], contract, preferred_element_type=jnp.float32)
        found += lax.dot_general(for_imag, held[1, rows, :], contract, preferred_element_type=jnp.float32)
        for piece, (at, width) in enumerate(lane_pieces(lines.shape[0] * LANES)):
            for part in range(2):
                to = pl.ds(part * GROUPS + group, count, stride=2 * GROUPS)
                filled = min(width, max(size - at, 0))
                if filled < width:
                    lines[piece, to, :] = jnp.zeros((count, width), jnp.float32)
                if filled > 0:
                    lines[piece, to, :filled] = found[part * count:(part + 1) * count, at:at + filled]
    for piece in range(lines.shape[0]):
        block = lines[piece].reshape(count, 2 * GROUPS, LANES)
        keep_ref[:, :, piece * LANES:(piece + 1) * LANES] = block[:half]
        send_ref[:, :, piece * LANES:(piece + 1) * LANES] = block[half:].astype(jnp.bfloat16)
    early.wait()


def transform(visibilities, beam, m_order, slot, order):
    rows, times = visibilities.shape[1:]
    count = m_order.shape[0]
    spans = group_spans(rows)
    width = padded(max(size for _, size in spans))

    def body(slot_ref, *refs):
        transform_kernel(spans, order, slot_ref[0], *refs)

    return pl.pallas_call(
        body,
        out_shape=[pltpu.VMEM((count // 2, 2 * GROUPS, width), kind) for kind in (jnp.float32, jnp.bfloat16)]
        + [pltpu.VMEM((beam.shape[0] // 2, beam.shape[1]), jnp.bfloat16)],
        in_specs=[
            pl.BlockSpec(memory_space=pltpu.SMEM),
            pl.BlockSpec(memory_space=pltpu.HBM),
            pl.BlockSpec(memory_space=pltpu.HBM),
            pl.BlockSpec(memory_space=pltpu.HBM),
        ],
        out_specs=[pl.BlockSpec(memory_space=pltpu.VMEM)] * 3,
        scratch_shapes=[
            pltpu.VMEM((2, rows, times), jnp.bfloat16),
            pltpu.VMEM((width // LANES, count * 2 * GROUPS, LANES), jnp.float32),
            pltpu.SMEM((count,), jnp.int32),
            pltpu.SemaphoreType.DMA((GROUPS + 2,)),
        ],
        compiler_params=pltpu.CompilerParams(vmem_limit_bytes=24 * MIB),
        name="transform",
    )(
        slot.reshape(1),
        *(pltpu.with_memory_space_constraint(given, pltpu.HBM) for given in (m_order, visibilities, beam)),
    )


def three_pieces(value):
    first = value.astype(jnp.bfloat16)
    rest = value - first.astype(jnp.float32)
    second = rest.astype(jnp.bfloat16)
    third = (rest - second.astype(jnp.float32)).astype(jnp.bfloat16)
    return [first, second, third]


def factor_kernel(
    spans, eager, given_pairs, given_gains, beam_ref, out_ref, early_ref, pairs_ref, gains_ref, sems
):
    fetches = [
        pltpu.make_async_copy(given_pairs, pairs_ref, sems.at[0]),
        pltpu.make_async_copy(given_gains, gains_ref, sems.at[1]),
    ]
    for fetch in fetches:
        fetch.start()
    early = pltpu.make_async_copy(beam_ref.at[pl.ds(early_ref.shape[0], early_ref.shape[0]), :], early_ref, sems.at[2])

    @pl.when(eager)
    def start_early():
        early.start()

    for fetch in fetches:
        fetch.wait()
    feeds = gains_ref.shape[1]
    tiles = feeds // LANES
    table = jnp.concatenate(
        [gains_ref[part:part + 1, tile * LANES:(tile + 1) * LANES] for part in range(2) for tile in range(tiles)], axis=0
    )
    pieces = jnp.concatenate(three_pieces(table), axis=0)
    tall = 2 * tiles
    out_ref[...] = jnp.zeros_like(out_ref)
    for group, (start, size) in enumerate(spans):
        picked = []
        for side in range(2):
            feed = pairs_ref[side:side + 1, pl.ds(start, size)]
            lane = jnp.bitwise_and(feed, LANES - 1)
            tile = lax.shift_right_logical(feed, LANES.bit_length() - 1)
            lane_iota = lax.broadcasted_iota(jnp.int32, (LANES, size), 0)
            one_hot = jnp.where(lane_iota == lane, 1.0, 0.0).astype(jnp.bfloat16)
            rows = jnp.dot(pieces, one_hot, preferred_element_type=jnp.float32)
            whole = (rows[:tall] + rows[tall:2 * tall]) + rows[2 * tall:]
            chosen = lax.broadcasted_iota(jnp.int32, (tiles, size), 0) == tile
            for part in range(2):
                picked.append(jnp.sum(jnp.where(chosen, whole[part * tiles:(part + 1) * tiles], 0.0), axis=0, keepdims=True))
        a_re, a_im, b_re, b_im = picked
        factor_re = a_re * b_re + a_im * b_im
        factor_im = a_im * b_re - a_re * b_im
        out_ref[0, group:group + 1, :size] = factor_re
        out_ref[0, GROUPS + group:GROUPS + group + 1, :size] = factor_re
        out_ref[1, group:group + 1, :size] = -factor_im
        out_ref[1, GROUPS + group:GROUPS + group + 1, :size] = factor_im

    @pl.when(eager)
    def finish_early():
        early.wait()


def factors(feed_pairs, feed_gains, beam, slot, eager_slots):
    rows, width = feed_pairs.shape[0], beam.shape[1]
    spans = group_spans(rows)
    line = padded(max(size for _, size in spans))

    def body(slot_ref, *refs):
        factor_kernel(spans, slot_ref[0] < eager_slots, *refs)

    return pl.pallas_call(
        body,
        out_shape=[
            pltpu.VMEM((2, 2 * GROUPS, line), jnp.float32),
            pltpu.VMEM((rows, width), jnp.bfloat16),
        ],
        in_specs=[pl.BlockSpec(memory_space=pltpu.SMEM)] + [pl.BlockSpec(memory_space=pltpu.HBM)] * 3,
        out_specs=[pl.BlockSpec(memory_space=pltpu.VMEM)] * 2,
        scratch_shapes=[
            pltpu.VMEM(feed_pairs.shape[::-1], jnp.int32),
            pltpu.VMEM(feed_gains.shape, jnp.float32),
            pltpu.SemaphoreType.DMA((3,)),
        ],
        cost_estimate=pl.CostEstimate(
            flops=2 * 2 * rows * 48 * 128, bytes_accessed=2 * rows * width + 8 * rows, transcendentals=0
        ),
        compiler_params=pltpu.CompilerParams(vmem_limit_bytes=16 * MIB),
        name="factors",
    )(
        slot.reshape(1),
        *(
            pltpu.with_memory_space_constraint(given, pltpu.HBM)
            for given in (jnp.transpose(feed_pairs), feed_gains, beam)
        ),
    )


def project_kernel(
    spans, share_order, eager, got_ref, factor_ref, first_ref, second_ref, beam_ref, out_ref, late_ref, partial, sems
):
    rows = first_ref.shape[0]
    late = [
        pltpu.make_async_copy(
            beam_ref.at[pl.ds(rows + start, size), :], late_ref.at[pl.ds(start, size), :], sems.at[group]
        )
        for group, (start, size) in enumerate(spans)
    ]

    @pl.when(jnp.logical_not(eager))
    def start_late():
        for copy in late:
            copy.start()

    total = got_ref[0].astype(jnp.float32)
    for source in range(1, got_ref.shape[0]):
        total += got_ref[source].astype(jnp.float32)
    swapped = jnp.concatenate([total[GROUPS:], total[:GROUPS]], axis=0)
    weighted = total * factor_ref[0] + swapped * factor_ref[1]
    high = weighted.astype(jnp.bfloat16)
    low = (weighted - high.astype(jnp.float32)).astype(jnp.bfloat16)
    rows16 = jnp.concatenate([high.astype(jnp.float32), low.astype(jnp.float32)], axis=0)
    row_group = jnp.bitwise_and(lax.broadcasted_iota(jnp.int32, rows16.shape, 0), GROUPS - 1)
    lefts = [jnp.where(row_group == group, rows16, 0.0).astype(jnp.bfloat16) for group in range(GROUPS)]

    def products(ref, copies):
        value = None
        for group, (start, size) in enumerate(spans):
            if copies:
                copies[group].wait()
            term = jnp.dot(
                lefts[group][:, :size], ref[pl.ds(start, size), :], preferred_element_type=jnp.float32
            )
            value = term if value is None else value + term
        return value

    def collected(value):
        value = value[:2 * GROUPS] + value[2 * GROUPS:]
        return [jnp.sum(value[piece * GROUPS:(piece + 1) * GROUPS], axis=0, keepdims=True) for piece in range(2)]

    sums = [collected(products(first_ref, None))]

    @pl.when(eager)
    def use_early():
        partial[...] = products(second_ref, None)

    @pl.when(jnp.logical_not(eager))
    def use_late():
        partial[...] = products(late_ref, late)

    sums.append(collected(partial[...]))
    answer = jnp.concatenate([sums[0][0] + sums[1][1], sums[0][1] - sums[1][0]], axis=0)
    width = answer.shape[1]
    share = width // len(share_order)
    for slab, k in enumerate(share_order):
        out_ref[slab, :, :share] = answer[:, k * share:(k + 1) * share]


def project(got, factor, first, second, beam, share_order, slot, eager_slots):
    rows, width = beam.shape
    spans = group_spans(rows // 2)

    def body(slot_ref, *refs):
        project_kernel(spans, share_order, slot_ref[0] < eager_slots, *refs)

    return pl.pallas_call(
        body,
        out_shape=jax.ShapeDtypeStruct((len(share_order), 2, padded(width // len(share_order))), jnp.float32),
        in_specs=[pl.BlockSpec(memory_space=pltpu.SMEM)]
        + [pl.BlockSpec(memory_space=pltpu.VMEM)] * 4
        + [pl.BlockSpec(memory_space=pltpu.HBM)],
        out_specs=pl.BlockSpec(memory_space=pltpu.VMEM),
        scratch_shapes=[
            pltpu.VMEM((rows // 2, width), jnp.bfloat16),
            pltpu.VMEM((4 * GROUPS, width), jnp.float32),
            pltpu.SemaphoreType.DMA((GROUPS,)),
        ],
        compiler_params=pltpu.CompilerParams(vmem_limit_bytes=16 * MIB),
        name="project",
    )(
        slot.reshape(1),
        *(pltpu.with_memory_space_constraint(held, pltpu.VMEM) for held in (got, factor, first, second)),
        pltpu.with_memory_space_constraint(beam, pltpu.HBM),
    )


def per_device(visibilities, beam_blocks, feed_pairs, feed_gains, m_order):
    shares = lax.axis_size("bl")
    slots = lax.axis_size("ma")
    share_width = beam_blocks.shape[3] // shares
    order = rotated(slots // 2, slots // 4)
    beam = beam_blocks.reshape(2 * beam_blocks.shape[2], beam_blocks.shape[3])
    slot = lax.axis_index("ma")
    keep, send, first = transform(visibilities, beam, m_order, slot, order)
    send, feed_gains = lax.optimization_barrier((send, feed_gains))
    factor, second = factors(feed_pairs, feed_gains, beam, slot, slots // 2)
    other = lax.ppermute(send, "ma", [(slot, slot ^ 1) for slot in range(slots)])
    pair, factor = lax.optimization_barrier(((keep + other.astype(jnp.float32)).astype(jnp.bfloat16), factor))
    same_core = [[2 * i + parity for i in order] for parity in range(2)]
    got = lax.all_to_all(pair, "ma", split_axis=0, concat_axis=0, tiled=True, axis_index_groups=same_core)
    share_order = rotated(shares, shares // 2 + 1)
    partial_modes = project(got, factor, first, second, beam, share_order, slot, slots // 2)
    parts = lax.all_to_all(
        partial_modes, "bl", split_axis=0, concat_axis=0, tiled=True, axis_index_groups=[share_order]
    )
    return jnp.sum(parts, axis=0)[:, None, :share_width]


def solution(mesh):
    return jax.shard_map(
        per_device,
        mesh=mesh,
        in_specs=(P(None, "bl", "ma"), P("ma", None, "bl", None), P("bl", None), P(), P()),
        out_specs=P(None, "ma", "bl"),
        check_vma=False,
    )
```

```python
import jax
import jax.numpy as jnp
from jax import lax
from jax.experimental import pallas as pl
from jax.experimental.pallas import tpu as pltpu
from jax.sharding import PartitionSpec as P

NT = 8192
GROUPS = 4
LANES = 128
MIB = 1024 * 1024


def group_spans(rows):
    step = rows // GROUPS // LANES * LANES
    starts = [group * step for group in range(GROUPS)]
    return [(start, (starts[i + 1] if i + 1 < GROUPS else rows) - start) for i, start in enumerate(starts)]


def rotated(count, first):
    return [(first + i) % count for i in range(count)]


def lane_pieces(size):
    return [(at, min(LANES, size - at)) for at in range(0, size, LANES)]


def padded(size):
    return -(-size // LANES) * LANES


def transform_kernel(
    spans, order, my_slot, given_m, vis_ref, beam_ref, keep_ref, send_ref, early_ref, held, lines, m_ref, sems
):
    fetch_m = pltpu.make_async_copy(given_m, m_ref, sems.at[GROUPS + 1])
    fetch_m.start()
    copies = []
    for group, (start, size) in enumerate(spans):
        rows = pl.ds(start, size)
        copy = pltpu.make_async_copy(vis_ref.at[:, rows, :], held.at[:, rows, :], sems.at[group])
        copy.start()
        copies.append(copy)
    early = pltpu.make_async_copy(beam_ref.at[pl.ds(0, early_ref.shape[0]), :], early_ref, sems.at[GROUPS])
    early.start()
    fetch_m.wait()
    count = m_ref.shape[0]
    half = count // 2
    times = vis_ref.shape[2]
    parity = jnp.bitwise_and(my_slot, 1)
    row = lax.broadcasted_iota(jnp.int32, (count, LANES), 0)
    m_values = jnp.zeros((count, LANES), jnp.int32)
    for i in range(half):
        m_values = jnp.where(row == i, m_ref[2 * order[i] + parity] - count // 2, m_values)
        m_values = jnp.where(row == half + i, m_ref[2 * order[i] + 1 - parity] - count // 2, m_values)
    begin = my_slot * times
    scale = 1.0 / jnp.sqrt(jnp.float32(NT))
    cos_parts, sin_parts = [], []
    for at in range(0, times, LANES):
        t = begin + at + lax.broadcasted_iota(jnp.int32, (count, LANES), 1)
        wrapped = jnp.bitwise_and(t * m_values, NT - 1).astype(jnp.float32)
        phases = wrapped * (2.0 * jnp.pi / NT)
        cos_parts.append(jnp.cos(phases) * scale)
        sin_parts.append(jnp.sin(phases) * scale)
    cos_part = jnp.concatenate(cos_parts, axis=1)
    sin_part = jnp.concatenate(sin_parts, axis=1)
    for_real = jnp.concatenate([cos_part, -sin_part], axis=0).astype(jnp.bfloat16)
    for_imag = jnp.concatenate([sin_part, cos_part], axis=0).astype(jnp.bfloat16)
    contract = (((1,), (1,)), ((), ()))
    for group, (start, size) in enumerate(spans):
        copies[group].wait()
        rows = pl.ds(start, size)
        found = lax.dot_general(for_real, held[0, rows, :], contract, preferred_element_type=jnp.float32)
        found += lax.dot_general(for_imag, held[1, rows, :], contract, preferred_element_type=jnp.float32)
        for piece, (at, width) in enumerate(lane_pieces(lines.shape[0] * LANES)):
            for part in range(2):
                to = pl.ds(part * GROUPS + group, half, stride=2 * GROUPS)
                filled = min(width, max(size - at, 0))
                kept = slice(part * count, part * count + half)
                sent = slice(part * count + half, (part + 1) * count)
                if filled < width:
                    lines[piece, to, :] = jnp.zeros((half, width), jnp.float32)
                    keep_ref[:, part * GROUPS + group, at:at + width] = jnp.zeros((half, width), jnp.float32)
                if filled > 0:
                    lines[piece, to, :filled] = found[sent, at:at + filled]
                    keep_ref[:, part * GROUPS + group, at:at + filled] = found[kept, at:at + filled]
    for piece in range(lines.shape[0]):
        block = lines[piece].reshape(half, 2 * GROUPS, LANES)
        send_ref[:, :, piece * LANES:(piece + 1) * LANES] = block.astype(jnp.bfloat16)
    early.wait()


def transform(visibilities, beam, m_order, slot, order):
    rows, times = visibilities.shape[1:]
    count = m_order.shape[0]
    spans = group_spans(rows)
    width = padded(max(size for _, size in spans))

    def body(slot_ref, *refs):
        transform_kernel(spans, order, slot_ref[0], *refs)

    return pl.pallas_call(
        body,
        out_shape=[pltpu.VMEM((count // 2, 2 * GROUPS, width), kind) for kind in (jnp.float32, jnp.bfloat16)]
        + [pltpu.VMEM((beam.shape[0] // 2, beam.shape[1]), jnp.bfloat16)],
        in_specs=[
            pl.BlockSpec(memory_space=pltpu.SMEM),
            pl.BlockSpec(memory_space=pltpu.HBM),
            pl.BlockSpec(memory_space=pltpu.HBM),
            pl.BlockSpec(memory_space=pltpu.HBM),
        ],
        out_specs=[pl.BlockSpec(memory_space=pltpu.VMEM)] * 3,
        scratch_shapes=[
            pltpu.VMEM((2, rows, times), jnp.bfloat16),
            pltpu.VMEM((width // LANES, count // 2 * 2 * GROUPS, LANES), jnp.float32),
            pltpu.SMEM((count,), jnp.int32),
            pltpu.SemaphoreType.DMA((GROUPS + 2,)),
        ],
        compiler_params=pltpu.CompilerParams(vmem_limit_bytes=24 * MIB),
        name="transform",
    )(
        slot.reshape(1),
        *(pltpu.with_memory_space_constraint(given, pltpu.HBM) for given in (m_order, visibilities, beam)),
    )


def three_pieces(value):
    first = value.astype(jnp.bfloat16)
    rest = value - first.astype(jnp.float32)
    second = rest.astype(jnp.bfloat16)
    third = (rest - second.astype(jnp.float32)).astype(jnp.bfloat16)
    return [first, second, third]


def factor_kernel(
    spans, eager, given_pairs, given_gains, beam_ref, out_ref, early_ref, pairs_ref, gains_ref, sems
):
    fetches = [
        pltpu.make_async_copy(given_pairs, pairs_ref, sems.at[0]),
        pltpu.make_async_copy(given_gains, gains_ref, sems.at[1]),
    ]
    for fetch in fetches:
        fetch.start()
    early = pltpu.make_async_copy(beam_ref.at[pl.ds(early_ref.shape[0], early_ref.shape[0]), :], early_ref, sems.at[2])

    @pl.when(eager)
    def start_early():
        early.start()

    for fetch in fetches:
        fetch.wait()
    feeds = gains_ref.shape[1]
    tiles = feeds // LANES
    table = jnp.concatenate(
        [gains_ref[part:part + 1, tile * LANES:(tile + 1) * LANES] for part in range(2) for tile in range(tiles)], axis=0
    )
    pieces = jnp.concatenate(three_pieces(table), axis=0)
    tall = 2 * tiles
    out_ref[...] = jnp.zeros_like(out_ref)
    for group, (start, size) in enumerate(spans):
        picked = []
        for side in range(2):
            feed = pairs_ref[side:side + 1, pl.ds(start, size)]
            lane = jnp.bitwise_and(feed, LANES - 1)
            tile = lax.shift_right_logical(feed, LANES.bit_length() - 1)
            lane_iota = lax.broadcasted_iota(jnp.int32, (LANES, size), 0)
            one_hot = jnp.where(lane_iota == lane, 1.0, 0.0).astype(jnp.bfloat16)
            rows = jnp.dot(pieces, one_hot, preferred_element_type=jnp.float32)
            whole = (rows[:tall] + rows[tall:2 * tall]) + rows[2 * tall:]
            chosen = lax.broadcasted_iota(jnp.int32, (tiles, size), 0) == tile
            for part in range(2):
                picked.append(jnp.sum(jnp.where(chosen, whole[part * tiles:(part + 1) * tiles], 0.0), axis=0, keepdims=True))
        a_re, a_im, b_re, b_im = picked
        factor_re = a_re * b_re + a_im * b_im
        factor_im = a_im * b_re - a_re * b_im
        out_ref[0, group:group + 1, :size] = factor_re
        out_ref[0, GROUPS + group:GROUPS + group + 1, :size] = factor_re
        out_ref[1, group:group + 1, :size] = -factor_im
        out_ref[1, GROUPS + group:GROUPS + group + 1, :size] = factor_im

    @pl.when(eager)
    def finish_early():
        early.wait()


def factors(feed_pairs, feed_gains, beam, slot, eager_slots):
    rows, width = feed_pairs.shape[0], beam.shape[1]
    spans = group_spans(rows)
    line = padded(max(size for _, size in spans))

    def body(slot_ref, *refs):
        factor_kernel(spans, slot_ref[0] < eager_slots, *refs)

    return pl.pallas_call(
        body,
        out_shape=[
            pltpu.VMEM((2, 2 * GROUPS, line), jnp.float32),
            pltpu.VMEM((rows, width), jnp.bfloat16),
        ],
        in_specs=[pl.BlockSpec(memory_space=pltpu.SMEM)] + [pl.BlockSpec(memory_space=pltpu.HBM)] * 3,
        out_specs=[pl.BlockSpec(memory_space=pltpu.VMEM)] * 2,
        scratch_shapes=[
            pltpu.VMEM(feed_pairs.shape[::-1], jnp.int32),
            pltpu.VMEM(feed_gains.shape, jnp.float32),
            pltpu.SemaphoreType.DMA((3,)),
        ],
        cost_estimate=pl.CostEstimate(
            flops=2 * 2 * rows * 48 * 128, bytes_accessed=2 * rows * width + 8 * rows, transcendentals=0
        ),
        compiler_params=pltpu.CompilerParams(vmem_limit_bytes=16 * MIB),
        name="factors",
    )(
        slot.reshape(1),
        *(
            pltpu.with_memory_space_constraint(given, pltpu.HBM)
            for given in (jnp.transpose(feed_pairs), feed_gains, beam)
        ),
    )


def project_kernel(
    spans, share_order, eager, got_ref, factor_ref, first_ref, second_ref, beam_ref, out_ref, late_ref, partial, sems
):
    rows = first_ref.shape[0]
    late = [
        pltpu.make_async_copy(
            beam_ref.at[pl.ds(rows + start, size), :], late_ref.at[pl.ds(start, size), :], sems.at[group]
        )
        for group, (start, size) in enumerate(spans)
    ]

    @pl.when(jnp.logical_not(eager))
    def start_late():
        for copy in late:
            copy.start()

    total = got_ref[0].astype(jnp.float32)
    for source in range(1, got_ref.shape[0]):
        total += got_ref[source].astype(jnp.float32)
    swapped = jnp.concatenate([total[GROUPS:], total[:GROUPS]], axis=0)
    weighted = total * factor_ref[0] + swapped * factor_ref[1]
    high = weighted.astype(jnp.bfloat16)
    low = (weighted - high.astype(jnp.float32)).astype(jnp.bfloat16)
    rows16 = jnp.concatenate([high.astype(jnp.float32), low.astype(jnp.float32)], axis=0)
    row_group = jnp.bitwise_and(lax.broadcasted_iota(jnp.int32, rows16.shape, 0), GROUPS - 1)
    lefts = [jnp.where(row_group == group, rows16, 0.0).astype(jnp.bfloat16) for group in range(GROUPS)]

    def products(ref, copies):
        value = None
        for group, (start, size) in enumerate(spans):
            if copies:
                copies[group].wait()
            term = jnp.dot(
                lefts[group][:, :size], ref[pl.ds(start, size), :], preferred_element_type=jnp.float32
            )
            value = term if value is None else value + term
        return value

    def collected(value):
        value = value[:2 * GROUPS] + value[2 * GROUPS:]
        return [jnp.sum(value[piece * GROUPS:(piece + 1) * GROUPS], axis=0, keepdims=True) for piece in range(2)]

    sums = [collected(products(first_ref, None))]

    @pl.when(eager)
    def use_early():
        partial[...] = products(second_ref, None)

    @pl.when(jnp.logical_not(eager))
    def use_late():
        partial[...] = products(late_ref, late)

    sums.append(collected(partial[...]))
    answer = jnp.concatenate([sums[0][0] + sums[1][1], sums[0][1] - sums[1][0]], axis=0)
    width = answer.shape[1]
    share = width // len(share_order)
    for slab, k in enumerate(share_order):
        out_ref[slab, :, :share] = answer[:, k * share:(k + 1) * share]


def project(got, factor, first, second, beam, share_order, slot, eager_slots):
    rows, width = beam.shape
    spans = group_spans(rows // 2)

    def body(slot_ref, *refs):
        project_kernel(spans, share_order, slot_ref[0] < eager_slots, *refs)

    return pl.pallas_call(
        body,
        out_shape=jax.ShapeDtypeStruct((len(share_order), 2, padded(width // len(share_order))), jnp.float32),
        in_specs=[pl.BlockSpec(memory_space=pltpu.SMEM)]
        + [pl.BlockSpec(memory_space=pltpu.VMEM)] * 4
        + [pl.BlockSpec(memory_space=pltpu.HBM)],
        out_specs=pl.BlockSpec(memory_space=pltpu.VMEM),
        scratch_shapes=[
            pltpu.VMEM((rows // 2, width), jnp.bfloat16),
            pltpu.VMEM((4 * GROUPS, width), jnp.float32),
            pltpu.SemaphoreType.DMA((GROUPS,)),
        ],
        compiler_params=pltpu.CompilerParams(vmem_limit_bytes=16 * MIB),
        name="project",
    )(
        slot.reshape(1),
        *(pltpu.with_memory_space_constraint(held, pltpu.VMEM) for held in (got, factor, first, second)),
        pltpu.with_memory_space_constraint(beam, pltpu.HBM),
    )


def per_device(visibilities, beam_blocks, feed_pairs, feed_gains, m_order):
    shares = lax.axis_size("bl")
    slots = lax.axis_size("ma")
    share_width = beam_blocks.shape[3] // shares
    order = rotated(slots // 2, slots // 4)
    beam = beam_blocks.reshape(2 * beam_blocks.shape[2], beam_blocks.shape[3])
    slot = lax.axis_index("ma")
    keep, send, first = transform(visibilities, beam, m_order, slot, order)
    send, feed_gains = lax.optimization_barrier((send, feed_gains))
    factor, second = factors(feed_pairs, feed_gains, beam, slot, slots // 2)
    other = lax.ppermute(send, "ma", [(slot, slot ^ 1) for slot in range(slots)])
    pair, factor = lax.optimization_barrier(((keep + other.astype(jnp.float32)).astype(jnp.bfloat16), factor))
    same_core = [[2 * i + parity for i in order] for parity in range(2)]
    got = lax.all_to_all(pair, "ma", split_axis=0, concat_axis=0, tiled=True, axis_index_groups=same_core)
    share_order = rotated(shares, shares // 2 + 1)
    partial_modes = project(got, factor, first, second, beam, share_order, slot, slots // 2)
    parts = lax.all_to_all(
        partial_modes, "bl", split_axis=0, concat_axis=0, tiled=True, axis_index_groups=[share_order]
    )
    return jnp.sum(parts, axis=0)[:, None, :share_width]


def solution(mesh):
    return jax.shard_map(
        per_device,
        mesh=mesh,
        in_specs=(P(None, "bl", "ma"), P("ma", None, "bl", None), P("bl", None), P(), P()),
        out_specs=P(None, "ma", "bl"),
        check_vma=False,
    )
```
